512 devices in a mesh: ctx: 64 (over z_lo, y, core), section: 2 (over z_hi), tp: 4 (over x).
Axes of the slice: x: 4, y: 4, z: 16 (z_hi: 2, z_lo: 8; z = z_hi * 8 + z_lo), core: 2. Of those that a mesh axis runs over, the one named last changes fastest.
Arguments:
- text_embed: bfloat16 [8192, 4096], P('ctx', ('section', 'tp')), may hold values from -6 to 6
- frame_feats: bfloat16 [8192, 1024], P('ctx', ('section', 'tp')), may hold values from -6 to 6
- frame_count: int32 [64], P('ctx'), may hold values from 0 to 128
- proj_weight: bfloat16 [1024, 4096], P(None, ('section', 'tp')), may hold values from -0.1875 to 0.1875
- norm_gain: bfloat16 [4096], replicated, may hold values from 0.099609375 to 1.8984375
- q_weight: bfloat16 [4096, 2048], P('ctx', ('section', 'tp')), may hold values from -0.046875 to 0.046875
- k_weight: bfloat16 [4096, 2048], P('ctx', ('section', 'tp')), may hold values from -0.046875 to 0.046875
- v_weight: bfloat16 [4096, 2048], P('ctx', ('section', 'tp')), may hold values from -0.09375 to 0.09375
Outputs:
- attended: bfloat16 [8192, 2048], P('ctx', ('section', 'tp'))
The draws below stay inside these ranges and needn't reach their ends.
All inputs are finite; a program needn't handle non-finite values.
Results may differ from the reference program's by a relative error of at most 0.012.
Values may be sent and summed in bfloat16 or wider, within the bound.
No kernel may reach another device: no remote copies, remote signals or barrier semaphores. Data moves between devices by JAX's collectives and lax.ppermute only.
A program may use at most 64 MiB of HBM per device.

```python
import math
import jax
import jax.numpy as jnp
from jax import lax

D = 4096
ROOT_D = 64
DV = 1024
HEADS = 16
HD = 128
TOK_DEV = 128
TOKENS = 8192
N_CTX = 64


def draw_text_embed(key, part):
    drawn = jnp.clip(jax.random.normal(jax.random.fold_in(key, 11), (TOKENS, D), jnp.float32), -6.0, 6.0)
    return drawn.astype(jnp.bfloat16)


def draw_q_weight(key, part):
    edge_value = 3.0 / ROOT_D
    drawn = jax.random.uniform(jax.random.fold_in(key, 21), (D, HEADS * HD), jnp.float32, -edge_value, edge_value)
    return drawn.astype(jnp.bfloat16)


def draw_k_weight(key, part):
    edge_value = 3.0 / ROOT_D
    drawn = jax.random.normal(jax.random.fold_in(key, 31), (D, HEADS * HD), jnp.float32) / ROOT_D
    drawn = jnp.clip(drawn, -edge_value, edge_value)
    return drawn.astype(jnp.bfloat16)


def plant(result, stream_key, low, high):
    shape = result.shape
    spot = [jax.random.randint(jax.random.fold_in(stream_key, axis), (), 0, shape[axis]) for axis in range(len(shape))]
    result = result.at[tuple(spot)].set(low)
    longest = shape.index(max(shape))
    spot[longest] = (spot[longest] + 1) % shape[longest]
    return result.at[tuple(spot)].set(high)


def block_scale(rng, extent, pieces, smallest, high):
    def one(position, parts):
        steps = jax.random.uniform(jax.random.fold_in(jax.random.fold_in(rng, 6), position), (parts,), jnp.float32, smallest / len(pieces), high / len(pieces))
        return jnp.repeat(jnp.exp(steps), extent[position] // parts).reshape((-1,) + (1,) * (len(extent) - position - 1))

    factor_of = one(*pieces[0])
    for cut in pieces[1:]:
        factor_of = factor_of * one(*cut)
    return factor_of


def scatter_about(stream_key, dims, width, limit, cuts=(), held_as=jnp.bfloat16):
    result = width * jax.random.normal(stream_key, dims, jnp.float32)
    if cuts:
        result = result * block_scale(stream_key, dims, cuts, -0.22, 0.18)
    return jnp.clip(result, -limit, limit).astype(held_as)


def setup_inputs(seed: int = 0) -> dict:
    key_of = jax.random.split(jax.random.key(seed), 9)
    return {
        "text_embed": draw_text_embed(jax.random.fold_in(key_of[8], 71), 0),
        "frame_feats": scatter_about(key_of[1], (TOKENS, DV), 1.0, 6.0, ((0, 64), (1, 8))),
        "frame_count": plant(jax.random.randint(key_of[2], (N_CTX,), 0, TOK_DEV + 1), jax.random.fold_in(key_of[2], 1), 0, TOK_DEV).astype(jnp.int32),
        "proj_weight": scatter_about(key_of[3], (DV, D), DV ** -0.5, 0.1875, ((1, 8),)),
        "norm_gain": jnp.clip(1.0 + 0.18 * jax.random.normal(key_of[4], (D,), jnp.float32), 0.099609375, 1.8984375).astype(jnp.bfloat16),
        "q_weight": draw_q_weight(jax.random.fold_in(key_of[8], 71), 0),
        "k_weight": draw_k_weight(jax.random.fold_in(key_of[8], 71), 0),
        "v_weight": scatter_about(key_of[7], (D, HEADS * HD), D ** -0.5, 0.09375, ((0, 64), (1, 8))),
    }


ROPE_BASE = 1000000.0
NORM_EPS = 1e-05
MASKED = -1e+30

def rotate(values, positions):
    half = values.shape[-1] // 2
    ladder = jnp.arange(half, dtype=jnp.float32) * 2.0 / values.shape[-1]
    freq = ROPE_BASE ** (-ladder)
    angle = positions.astype(jnp.float32)[:, None] * freq[None, :]
    cosine = jnp.cos(angle)[:, None, :]
    sine = jnp.sin(angle)[:, None, :]
    first = values[..., :half]
    second = values[..., half:]
    return jnp.concatenate([first * cosine - second * sine, second * cosine + first * sine], axis=-1)

def reference(text_embed, frame_feats, frame_count, proj_weight, norm_gain, q_weight, k_weight, v_weight):
    vision = jnp.dot(frame_feats, proj_weight, preferred_element_type=jnp.float32)
    places = jnp.arange(TOKENS, dtype=jnp.int32)
    blocks = places // TOK_DEV
    is_frame = places % TOK_DEV < frame_count[blocks]
    joined = jnp.where(is_frame[:, None], vision, text_embed.astype(jnp.float32)).astype(jnp.bfloat16)
    wide = joined.astype(jnp.float32)
    mean_square = lax.optimization_barrier(jnp.mean(wide * wide, axis=-1, keepdims=True))
    normed = (wide * lax.rsqrt(mean_square + NORM_EPS) * norm_gain.astype(jnp.float32)).astype(jnp.bfloat16)
    qlin = jnp.dot(normed, q_weight, preferred_element_type=jnp.float32)
    klin = jnp.dot(normed, k_weight, preferred_element_type=jnp.float32)
    vlin = jnp.dot(normed, v_weight, preferred_element_type=jnp.float32)
    queries = rotate(qlin.reshape(TOKENS, HEADS, HD), places).astype(jnp.bfloat16)
    keys = rotate(klin.reshape(TOKENS, HEADS, HD), places).astype(jnp.bfloat16)
    values = vlin.reshape(TOKENS, HEADS, HD).astype(jnp.bfloat16)
    scale = 1.0 / math.sqrt(HD)
    allowed = places[None, :] <= places[:, None]

    def one_head(items):
        query_head, key_head, value_head = items
        scores = jnp.dot(query_head, key_head.T, preferred_element_type=jnp.float32) * scale
        best = lax.optimization_barrier(jnp.max(jnp.where(allowed, scores, MASKED), axis=-1))
        weights = jnp.where(allowed, jnp.exp(scores - best[:, None]), 0.0)
        total = lax.optimization_barrier(jnp.sum(weights, axis=-1))
        product = jnp.dot(weights.astype(jnp.bfloat16), value_head, preferred_element_type=jnp.float32)
        return product / total[:, None]
    outputs = lax.map(one_head, (queries.transpose(1, 0, 2), keys.transpose(1, 0, 2), values.transpose(1, 0, 2)))
    return outputs.transpose(1, 0, 2).reshape(TOKENS, HEADS * HD).astype(jnp.bfloat16)
```

```python
import math

import jax
import jax.numpy as jnp
from jax import lax
from jax.sharding import Mesh, PartitionSpec as P

HD = 128
ROPE_BASE = 1000000.0
NORM_EPS = 1e-05
MASKED = -1e30

Z, Y, CORES, SECTIONS, TP = 8, 4, 2, 2, 4
F = ("section", "tp")


def gather(v, axes, n):
    return lax.all_to_all(
        jnp.broadcast_to(v[None], (n, *v.shape)), axes, split_axis=0, concat_axis=0, tiled=True
    )


def rotate(values, positions):
    half = values.shape[-1] // 2
    ladder = jnp.arange(half, dtype=jnp.float32) * 2.0 / values.shape[-1]
    freq = ROPE_BASE ** (-ladder)
    angle = positions.astype(jnp.float32)[:, None] * freq[None, :]
    cosine = jnp.cos(angle)
    sine = jnp.sin(angle)
    first = values[..., :half]
    second = values[..., half:]
    return jnp.concatenate(
        [first * cosine - second * sine, second * cosine + first * sine], axis=-1
    )


def local(text, feats, count, proj, gain, q_weight, k_weight, v_weight):
    rows = text.shape[0]
    z, y, core = lax.axis_index("z"), lax.axis_index("y"), lax.axis_index("core")

    weight = jnp.stack([q_weight, k_weight, v_weight], axis=1).reshape(64, 3, 2, HD)
    weight = weight.transpose(2, 0, 1, 3).reshape(2, 64, 3 * HD)
    weight = lax.all_to_all(weight, "core", 0, 0, tiled=True).reshape(128, 3 * HD)
    weight = gather(weight, "z", Z)
    weight = gather(weight, "y", Y)

    feats_all = gather(feats, F, 8)
    vision = jnp.einsum(
        "frk,fkn->rn", feats_all, proj.reshape(8, 128, 512), preferred_element_type=jnp.float32
    )
    is_frame = jnp.arange(rows, dtype=jnp.int32) < count[0]
    joined = jnp.where(is_frame[:, None], vision, text.astype(jnp.float32)).astype(jnp.bfloat16)

    swapped = gather(joined, "section", SECTIONS)
    whole = gather(swapped, "tp", TP)
    whole = gather(whole, "core", CORES)
    whole = whole.transpose(0, 3, 2, 1, 4).reshape(2 * rows, 4096)
    wide = whole.astype(jnp.float32)
    mean_square = jnp.mean(wide * wide, axis=-1, keepdims=True)
    normed = (wide * lax.rsqrt(mean_square + NORM_EPS) * gain.astype(jnp.float32)).astype(
        jnp.bfloat16
    )
    qkv = jnp.einsum(
        "rzyk,yzkn->rn",
        normed.reshape(2 * rows, Z, Y, HD),
        weight.reshape(Y, Z, HD, 3 * HD),
        preferred_element_type=jnp.float32,
    )
    chip_rows = 2 * rows
    pos = (z * Y + y) * chip_rows + jnp.arange(chip_rows, dtype=jnp.int32)
    queries = rotate(qkv[:, :HD], pos).astype(jnp.bfloat16)
    keys = rotate(qkv[:, HD : 2 * HD], pos).astype(jnp.bfloat16)
    values = qkv[:, 2 * HD :].astype(jnp.bfloat16)

    kv = gather(jnp.concatenate([keys, values], axis=1), "z", Z).reshape(Z * chip_rows, 2 * HD)
    q_all = gather(queries, "y", Y).reshape(Y * chip_rows, HD)
    q_pos = z * (Y * chip_rows) + jnp.arange(Y * chip_rows, dtype=jnp.int32)
    k_pos = (
        jnp.arange(Z, dtype=jnp.int32)[:, None] * (Y * chip_rows)
        + y * chip_rows
        + jnp.arange(chip_rows, dtype=jnp.int32)[None, :]
    ).reshape(-1)
    scores = jnp.dot(q_all, kv[:, :HD].T, preferred_element_type=jnp.float32) / math.sqrt(HD)
    allowed = k_pos[None, :] <= q_pos[:, None]
    best = jnp.max(jnp.where(allowed, scores, MASKED), axis=-1)
    weights = jnp.where(allowed, jnp.exp(scores - best[:, None]), 0.0)
    total = jnp.sum(weights, axis=-1)
    product = jnp.dot(weights.astype(jnp.bfloat16), kv[:, HD:], preferred_element_type=jnp.float32)
    part = product / jnp.where(total > 0.0, total, 1.0)[:, None]
    lse = jnp.where(total > 0.0, best + jnp.log(jnp.where(total > 0.0, total, 1.0)), MASKED)

    parts = lax.all_to_all(
        part.astype(jnp.bfloat16).reshape(Y, chip_rows, HD), "y", 0, 0, tiled=True
    )
    lses = lax.all_to_all(lse.reshape(Y, 2, HD), "y", 0, 0, tiled=True).reshape(Y, chip_rows)
    top = jnp.max(lses, axis=0)
    share = jnp.exp(lses - top)
    share = share / jnp.sum(share, axis=0)
    result = jnp.sum(parts.astype(jnp.float32) * share[..., None], axis=0).astype(jnp.bfloat16)

    result = lax.all_to_all(result.reshape(2, rows, HD), "core", 0, 0, tiled=True)
    return result.transpose(1, 0, 2).reshape(rows, 2 * HD)


def solution(mesh):
    fine = Mesh(
        mesh.devices.reshape(Z, Y, CORES, SECTIONS, TP), ("z", "y", "core", "section", "tp")
    )
    ctx = ("z", "y", "core")
    in_specs = (P(ctx, F), P(ctx, F), P(ctx), P(None, F), P(), P(ctx, F), P(ctx, F), P(ctx, F))
    return jax.shard_map(
        local, mesh=fine, in_specs=in_specs, out_specs=P(ctx, F), check_vma=False
    )
```

```python
import math

import jax
import jax.numpy as jnp
from jax import lax
from jax.experimental import pallas as pl
from jax.experimental.pallas import tpu as pltpu
from jax.sharding import Mesh, PartitionSpec as P

HD = 128
ROPE_BASE = 1000000.0
NORM_EPS = 1e-05
MASKED = -1e30

ZH, ZL, Y, CORES, SECTIONS, TP = 2, 4, 4, 2, 2, 4
F = ("section", "tp")
ROWS = 128
CHIP_ROWS = 2 * ROWS
SWAP = [(0, 1), (1, 0)]
VMEM = pl.BlockSpec(memory_space=pltpu.VMEM)
SMEM = pl.BlockSpec(memory_space=pltpu.SMEM)
LIMIT = 40 << 20


def swap(v, axis):
    return lax.ppermute(v, axis, SWAP)


def gather(v, axis, n):
    return lax.all_to_all(jnp.broadcast_to(v[None], (n, *v.shape)), axis, 0, 0, tiled=True)


def join_frames_kernel(pick, feats, proj, text, out):
    vision = jnp.zeros((ROWS, 512), jnp.float32)
    for s in range(SECTIONS):
        first = jnp.bitwise_xor(pick[0], s) * TP
        for t in range(TP):
            vision = vision + jnp.dot(
                feats[t, s], proj[first + t], preferred_element_type=jnp.float32
            )
    row = lax.broadcasted_iota(jnp.int32, (ROWS, 512), 0)
    joined = jnp.where(row < pick[1], vision, text[...].astype(jnp.float32))
    out[...] = joined.astype(jnp.bfloat16)


def project_kernel(
    flip, own_a, own_b, other_a, other_b, stored, gain, cosine, sine, q_out, kv_out, weight, sem
):
    copy = pltpu.make_async_copy(stored, weight, sem)
    copy.start()
    tiles = [(own, other, t) for own, other in ((own_a, other_a), (own_b, other_b)) for t in range(TP)]
    squares = jnp.zeros((CHIP_ROWS, 512), jnp.float32)
    for own, other, t in tiles:
        wide = jnp.concatenate([own[t], other[t]], axis=0).astype(jnp.float32)
        squares = squares + wide * wide
    mean_square = jnp.sum(squares, axis=-1, keepdims=True) * (1.0 / 4096)
    inverse = lax.rsqrt(mean_square + NORM_EPS)
    total = jnp.zeros((CHIP_ROWS, 3 * HD), jnp.float32)
    copy.wait()
    for i, (own, other, t) in enumerate(tiles):
        half = jnp.bitwise_xor(flip[0], i // TP)
        wide = jnp.concatenate([own[t], other[t]], axis=0).astype(jnp.float32)
        normed = (wide * inverse * gain[i : i + 1, :]).astype(jnp.bfloat16)
        block = jnp.concatenate(
            [weight[y, t * CORES + c, half] for y in range(Y) for c in range(CORES)], axis=0
        )
        total = total + jnp.dot(normed, block, preferred_element_type=jnp.float32)
    q = total[:, :HD]
    k = total[:, HD : 2 * HD]
    cos, sin = cosine[...], sine[...]
    q = (q * cos + pltpu.roll(q, HD // 2, 1) * sin).astype(jnp.bfloat16)
    for i in range(Y):
        q_out[i] = q
    kv_out[:, :HD] = (k * cos + pltpu.roll(k, HD // 2, 1) * sin).astype(jnp.bfloat16)
    kv_out[:, HD:] = total[:, 2 * HD :].astype(jnp.bfloat16)


def encode(level):
    lane = lax.broadcasted_iota(jnp.int32, (CHIP_ROWS, HD), 1)
    high = level.astype(jnp.bfloat16).astype(jnp.float32)
    rest = level - high
    middle = rest.astype(jnp.bfloat16).astype(jnp.float32)
    low = rest - middle
    coded = jnp.where(
        lane == 0, high, jnp.where(lane == 1, middle, jnp.where(lane == 2, low, 0.0))
    ).astype(jnp.bfloat16)
    pick = lax.broadcasted_iota(jnp.int32, (8, HD), 0) == lax.broadcasted_iota(jnp.int32, (8, HD), 1)
    pick = pick.astype(jnp.float32).astype(jnp.bfloat16)
    coded = lax.dot_general(
        pick, coded, (((1,), (1,)), ((), ())), preferred_element_type=jnp.float32
    )
    return jnp.concatenate([coded[:, :ROWS], coded[:, ROWS:]], axis=0).astype(jnp.bfloat16)


def decode(coded):
    shape = (ROWS, ROWS)
    eye = lax.broadcasted_iota(jnp.int32, shape, 0) == lax.broadcasted_iota(jnp.int32, shape, 1)
    eye = eye.astype(jnp.float32).astype(jnp.bfloat16)
    c = lax.dot_general(eye, coded, (((1,), (1,)), ((), ())), preferred_element_type=jnp.float32)
    return c[:, 0:1] + c[:, 1:2] + c[:, 2:3]


def attend_kernel(place, queries, kv, out, scores):
    zh, zl, me, core = place[0], place[1], place[2], place[3]
    shape = (CHIP_ROWS, CHIP_ROWS)
    turn = core * ROWS
    row = jnp.bitwise_xor(lax.broadcasted_iota(jnp.int32, shape, 0), turn)
    col = jnp.bitwise_xor(lax.broadcasted_iota(jnp.int32, shape, 1), turn)
    ahead = col - row
    scale = 1.0 / math.sqrt(HD)

    def one(y, carry):
        q = queries[y]
        first_q = (zh * ZL + zl) * (Y * CHIP_ROWS) + y * CHIP_ROWS
        peak = jnp.full(shape, MASKED, jnp.float32)
        for l in range(ZL):
            for h in range(ZH):
                first_k = (jnp.bitwise_xor(zh, h) * ZL + l) * (Y * CHIP_ROWS) + me * CHIP_ROWS
                s = lax.dot_general(
                    q,
                    kv[l, h, :, :HD],
                    (((1,), (1,)), ((), ())),
                    preferred_element_type=jnp.float32,
                )
                s = jnp.where(ahead <= first_q - first_k, s * scale, MASKED)
                scores[l * ZH + h] = s
                peak = jnp.maximum(peak, s)
        best = jnp.max(peak, axis=-1, keepdims=True)
        mass = jnp.zeros(shape, jnp.float32)
        part = jnp.zeros((CHIP_ROWS, HD), jnp.float32)
        for l in range(ZL):
            for h in range(ZH):
                w = jnp.exp(scores[l * ZH + h] - best)
                mass = mass + w
                part = part + jnp.dot(
                    w.astype(jnp.bfloat16), kv[l, h, :, HD:], preferred_element_type=jnp.float32
                )
        total = jnp.sum(mass, axis=-1, keepdims=True)
        level = jnp.where(best > 0.5 * MASKED, best + jnp.log(total), MASKED)
        coded = encode(level)
        part = (part / total).astype(jnp.bfloat16)
        for i in range(CORES):
            owner = y * CORES + jnp.bitwise_xor(core, i)
            out[owner, :ROWS, :] = part[i * ROWS : (i + 1) * ROWS]
            out[owner, ROWS:, :] = coded[i * 8 : (i + 1) * 8]
        return carry

    lax.fori_loop(0, Y, one, 0)


def merge_kernel(parts, out):
    for h in range(CORES):
        blocks = [parts[y * CORES + h] for y in range(Y)]
        levels = [decode(block[ROWS:, :]) for block in blocks]
        top = jnp.maximum(jnp.maximum(levels[0], levels[1]), jnp.maximum(levels[2], levels[3]))
        total = jnp.zeros_like(top)
        result = jnp.zeros((ROWS, HD), jnp.float32)
        for level, block in zip(levels, blocks):
            share = jnp.exp(level - top)
            total = total + share
            result = result + share * block[:ROWS, :].astype(jnp.float32)
        out[:, h * HD : (h + 1) * HD] = (result / total).astype(jnp.bfloat16)


def join_kernel(q, k, v, out, sems):
    copies = [
        pltpu.make_async_copy(w, out.at[:, i * 2 * HD : (i + 1) * 2 * HD], sems.at[i])
        for i, w in enumerate((q, k, v))
    ]
    for copy in copies:
        copy.start()
    for copy in copies:
        copy.wait()


def spread_kernel(own, partner, out):
    for h in range(CORES):
        for zr, w in enumerate((own, partner)):
            for i in range(3):
                block = w[:, (2 * i + h) * HD : (2 * i + h + 1) * HD]
                for l in range(ZL):
                    out[l * CORES + h, zr, :, i * HD : (i + 1) * HD] = block


def call(kernel, outs, n_scalars, n_arrays, flops, size, scratch=()):
    return pl.pallas_call(
        kernel,
        out_shape=outs,
        in_specs=[SMEM] * n_scalars + [VMEM] * n_arrays,
        out_specs=[VMEM] * len(outs),
        scratch_shapes=list(scratch),
        compiler_params=pltpu.CompilerParams(vmem_limit_bytes=LIMIT),
        cost_estimate=pl.CostEstimate(flops=flops, bytes_accessed=size, transcendentals=0),
    )


def shaped(*shape):
    return jax.ShapeDtypeStruct(shape, jnp.bfloat16)


def local(text, feats, count, proj, gain, q_weight, k_weight, v_weight):
    zh, zl, y = lax.axis_index("zh"), lax.axis_index("zl"), lax.axis_index("y")
    core, section = lax.axis_index("core"), lax.axis_index("section")

    turned = jnp.bitwise_xor(jnp.arange(CHIP_ROWS, dtype=jnp.int32), core * ROWS)
    position = ((zh * ZL + zl) * Y + y) * CHIP_ROWS + turned
    ladder = jnp.arange(HD // 2, dtype=jnp.float32) * 2.0 / HD
    angle = position.astype(jnp.float32)[:, None] * (ROPE_BASE ** (-ladder))[None, :]
    cosine = jnp.cos(angle)
    sine = jnp.sin(angle)
    cosine = jnp.concatenate([cosine, cosine], axis=-1)
    sine = jnp.concatenate([-sine, sine], axis=-1)
    gains = gain.astype(jnp.float32).reshape(SECTIONS, TP, 512)
    gains = jnp.where(section == 0, gains, gains[::-1]).reshape(8, 512)
    feats_b = swap(feats, "section")
    weight = pl.pallas_call(
        join_kernel,
        out_shape=shaped(64, 6 * HD),
        in_specs=[pl.BlockSpec(memory_space=pl.ANY)] * 3,
        out_specs=VMEM,
        scratch_shapes=[pltpu.SemaphoreType.DMA((3,))],
        cost_estimate=pl.CostEstimate(flops=0, bytes_accessed=200000, transcendentals=0),
    )(q_weight, k_weight, v_weight)
    weight_b = swap(weight, "zh")

    weight_b, feats_b = lax.optimization_barrier((weight_b, feats_b))
    (weight,) = call(spread_kernel, [shaped(ZL * CORES, ZH, 64, 3 * HD)], 0, 2, 1000, 1 << 20)(
        weight, weight_b
    )
    weight = lax.all_to_all(weight, ("zl", "core"), 0, 0, tiled=True)

    feats = lax.all_gather(jnp.stack([feats, feats_b]), "tp", axis=0)
    (joined,) = call(join_frames_kernel, [shaped(ROWS, 512)], 1, 3, 2 * ROWS * 1024 * 512, 2 << 20)(
        jnp.stack([section, count[0]]), feats, proj.reshape(8, HD, 512), text
    )

    weight, joined = lax.optimization_barrier((weight, joined))
    weight = lax.all_gather(weight, "y", axis=0)
    joined_b = swap(joined, "section")
    own_a = lax.all_gather(joined, "tp", axis=0)
    own_a, joined_b = lax.optimization_barrier((own_a, joined_b))
    other_a = swap(own_a, "core")
    own_b = gather(joined_b, "tp", TP)
    other_b = swap(own_b, "core")
    queries, kv = pl.pallas_call(
        project_kernel,
        out_shape=[shaped(Y, CHIP_ROWS, HD), shaped(CHIP_ROWS, 2 * HD)],
        in_specs=[SMEM] + [VMEM] * 4 + [pl.BlockSpec(memory_space=pltpu.HBM)] + [VMEM] * 3,
        out_specs=[VMEM, VMEM],
        scratch_shapes=[
            pltpu.VMEM((Y, ZL * CORES, ZH, 64, 3 * HD), jnp.bfloat16),
            pltpu.SemaphoreType.DMA,
        ],
        compiler_params=pltpu.CompilerParams(vmem_limit_bytes=LIMIT),
        cost_estimate=pl.CostEstimate(
            flops=2 * CHIP_ROWS * 4096 * 3 * HD, bytes_accessed=6 << 20, transcendentals=0
        ),
    )(
        jnp.bitwise_xor(zh, section).reshape(1),
        own_a,
        own_b,
        other_a,
        other_b,
        pltpu.with_memory_space_constraint(weight, pltpu.HBM),
        gains,
        cosine,
        sine,
    )

    kv_b = swap(kv, "zh")
    queries = lax.all_to_all(queries, "y", 0, 0, tiled=True)
    kv = gather(jnp.stack([kv, kv_b]), "zl", ZL)
    (parts,) = call(
        attend_kernel,
        [shaped(Y * CORES, ROWS + 8, HD)],
        1,
        2,
        4 * 1024 * 2048 * HD,
        2 << 20,
        [pltpu.VMEM((ZL * ZH, CHIP_ROWS, CHIP_ROWS), jnp.float32)],
    )(jnp.stack([zh, zl, y, core]), queries, kv)

    parts = lax.all_to_all(parts, ("y", "core"), 0, 0, tiled=True)
    (result,) = call(merge_kernel, [shaped(ROWS, 2 * HD)], 0, 1, 1 << 20, 1 << 20)(parts)
    return result


def solution(mesh):
    fine = Mesh(
        mesh.devices.reshape(ZH, ZL, Y, CORES, SECTIONS, TP),
        ("zh", "zl", "y", "core", "section", "tp"),
    )
    ctx = ("zh", "zl", "y", "core")
    in_specs = (P(ctx, F), P(ctx, F), P(ctx), P(None, F), P(), P(ctx, F), P(ctx, F), P(ctx, F))
    return jax.shard_map(
        local, mesh=fine, in_specs=in_specs, out_specs=P(ctx, F), check_vma=False
    )
```

```python
import math

import jax
import jax.numpy as jnp
from jax import lax
from jax.experimental import pallas as pl
from jax.experimental.pallas import tpu as pltpu
from jax.sharding import Mesh, PartitionSpec as P

HD = 128
ROPE_BASE = 1000000.0
NORM_EPS = 1e-05
MASKED = -1e30

ZH, ZL, Y, CORES, SECTIONS, TP = 2, 4, 4, 2, 2, 4
F = ("section", "tp")
ROWS = 128
CHIP_ROWS = 2 * ROWS
SWAP = [(0, 1), (1, 0)]
VMEM = pl.BlockSpec(memory_space=pltpu.VMEM)
SMEM = pl.BlockSpec(memory_space=pltpu.SMEM)
LIMIT = 40 << 20


def swap(v, axis):
    return lax.ppermute(v, axis, SWAP)


def gather(v, axis, n):
    return lax.all_to_all(jnp.broadcast_to(v[None], (n, *v.shape)), axis, 0, 0, tiled=True)


def join_frames_kernel(pick, feats, proj, text, out):
    vision = jnp.zeros((ROWS, 512), jnp.float32)
    for s in range(SECTIONS):
        first = jnp.bitwise_xor(pick[0], s) * TP
        for t in range(TP):
            vision = vision + jnp.dot(
                feats[t, s], proj[first + t], preferred_element_type=jnp.float32
            )
    row = lax.broadcasted_iota(jnp.int32, (ROWS, 512), 0)
    joined = jnp.where(row < pick[1], vision, text[...].astype(jnp.float32))
    out[...] = joined.astype(jnp.bfloat16)


def project_kernel(
    flip, own_a, own_b, other_a, other_b, stored, gain, cosine, sine, q_out, kv_out, lines_out, weight, sem
):
    copies = [
        pltpu.make_async_copy(
            stored.at[:, t * CORES : (t + 1) * CORES], weight.at[:, t * CORES : (t + 1) * CORES], sem.at[t]
        )
        for t in range(TP)
    ]
    for copy in copies:
        copy.start()
    tiles = [(own, other, t) for own, other in ((own_a, other_a), (own_b, other_b)) for t in range(TP)]
    squares = jnp.zeros((CHIP_ROWS, 512), jnp.float32)
    for own, other, t in tiles:
        wide = jnp.concatenate([own[t], other[t]], axis=0).astype(jnp.float32)
        squares = squares + wide * wide
    mean_square = jnp.sum(squares, axis=-1, keepdims=True) * (1.0 / 4096)
    inverse = lax.rsqrt(mean_square + NORM_EPS)
    total = jnp.zeros((CHIP_ROWS, 3 * HD), jnp.float32)
    for i, (own, other, t) in enumerate(tiles):
        if i < TP:
            copies[i].wait()
        half = jnp.bitwise_xor(flip[0], i // TP)
        wide = jnp.concatenate([own[t], other[t]], axis=0).astype(jnp.float32)
        normed = (wide * inverse * gain[i : i + 1, :]).astype(jnp.bfloat16)
        block = jnp.concatenate(
            [weight[y, t * CORES + c, half] for y in range(Y) for c in range(CORES)], axis=0
        )
        total = total + jnp.dot(normed, block, preferred_element_type=jnp.float32)
    q = total[:, :HD]
    k = total[:, HD : 2 * HD]
    cos, sin = cosine[...], sine[...]
    q_out[...] = (q * cos + pltpu.roll(q, HD // 2, 1) * sin).astype(jnp.bfloat16)
    k = (k * cos + pltpu.roll(k, HD // 2, 1) * sin).astype(jnp.bfloat16)
    v = total[:, 2 * HD :].astype(jnp.bfloat16)
    kv_out[:, :HD] = k
    kv_out[:, HD:] = v
    for i in range(ZL):
        lines_out[i, :, :HD] = k
        lines_out[i, :, HD:] = v


def encode(level):
    lane = lax.broadcasted_iota(jnp.int32, (CHIP_ROWS, HD), 1)
    high = level.astype(jnp.bfloat16).astype(jnp.float32)
    rest = level - high
    middle = rest.astype(jnp.bfloat16).astype(jnp.float32)
    low = rest - middle
    coded = jnp.where(
        lane == 0, high, jnp.where(lane == 1, middle, jnp.where(lane == 2, low, 0.0))
    ).astype(jnp.bfloat16)
    pick = lax.broadcasted_iota(jnp.int32, (8, HD), 0) == lax.broadcasted_iota(jnp.int32, (8, HD), 1)
    pick = pick.astype(jnp.float32).astype(jnp.bfloat16)
    coded = lax.dot_general(
        pick, coded, (((1,), (1,)), ((), ())), preferred_element_type=jnp.float32
    )
    return jnp.concatenate([coded[:, :ROWS], coded[:, ROWS:]], axis=0).astype(jnp.bfloat16)


def decode(coded):
    shape = (ROWS, ROWS)
    eye = lax.broadcasted_iota(jnp.int32, shape, 0) == lax.broadcasted_iota(jnp.int32, shape, 1)
    eye = eye.astype(jnp.float32).astype(jnp.bfloat16)
    c = lax.dot_general(eye, coded, (((1,), (1,)), ((), ())), preferred_element_type=jnp.float32)
    return c[:, 0:1] + c[:, 1:2] + c[:, 2:3]


def attend(q, kv, scores, mask):
    shape = (CHIP_ROWS, CHIP_ROWS)
    scale = 1.0 / math.sqrt(HD)
    peak = jnp.full(shape, MASKED, jnp.float32)
    for l in range(ZL):
        s = lax.dot_general(
            q, kv[l, :, :HD], (((1,), (1,)), ((), ())), preferred_element_type=jnp.float32
        )
        s = mask(l, s * scale)
        scores[l] = s
        peak = jnp.maximum(peak, s)
    best = jnp.max(peak, axis=-1, keepdims=True)
    mass = jnp.zeros(shape, jnp.float32)
    part = jnp.zeros((CHIP_ROWS, HD), jnp.float32)
    for l in range(ZL):
        w = jnp.exp(scores[l] - best)
        mass = mass + w
        part = part + jnp.dot(
            w.astype(jnp.bfloat16), kv[l, :, HD:], preferred_element_type=jnp.float32
        )
    total = jnp.sum(mass, axis=-1, keepdims=True)
    return part / total, jnp.where(best > 0.5 * MASKED, best + jnp.log(total), MASKED)


def attend_own_kernel(place, queries, kv, parts, levels, scores):
    zl, me, core = place[1], place[2], place[3]
    shape = (CHIP_ROWS, CHIP_ROWS)
    turn = core * ROWS
    row = jnp.bitwise_xor(lax.broadcasted_iota(jnp.int32, shape, 0), turn)
    col = jnp.bitwise_xor(lax.broadcasted_iota(jnp.int32, shape, 1), turn)
    ahead = col - row

    def one(pair, carry):
        for i in range(2):
            y = pair * 2 + i

            def mask(l, s):
                return jnp.where(ahead <= ((zl - l) * Y + y - me) * CHIP_ROWS, s, MASKED)

            part, level = attend(queries[y], kv, scores.at[i], mask)
            parts[y] = part
            levels[y] = jnp.broadcast_to(level, (CHIP_ROWS, HD))
        return carry

    lax.fori_loop(0, Y // 2, one, 0)


def attend_rest_kernel(place, queries, kv, parts, levels, out, scores):
    def put(y, part, level):
        coded = encode(level)
        part = part.astype(jnp.bfloat16)
        for i in range(CORES):
            owner = y * CORES + jnp.bitwise_xor(place[3], i)
            out[owner, :ROWS, :] = part[i * ROWS : (i + 1) * ROWS]
            out[owner, ROWS:, :] = coded[i * 8 : (i + 1) * 8]

    @pl.when(place[0] == 0)
    def _():
        for y in range(Y):
            put(y, parts[y], levels[y, :, 0:1])

    @pl.when(place[0] != 0)
    def _():
        def one(pair, carry):
            for i in range(2):
                y = pair * 2 + i
                part, level = attend(queries[y], kv, scores.at[i], lambda l, s: s)
                before = levels[y, :, 0:1]
                top = jnp.maximum(level, before)
                new, old = jnp.exp(level - top), jnp.exp(before - top)
                total = new + old
                put(y, (part * new + parts[y] * old) / total, top + jnp.log(total))
            return carry

        lax.fori_loop(0, Y // 2, one, 0)


def merge_kernel(parts, out):
    for h in range(CORES):
        blocks = [parts[y * CORES + h] for y in range(Y)]
        levels = [decode(block[ROWS:, :]) for block in blocks]
        top = jnp.maximum(jnp.maximum(levels[0], levels[1]), jnp.maximum(levels[2], levels[3]))
        total = jnp.zeros_like(top)
        result = jnp.zeros((ROWS, HD), jnp.float32)
        for level, block in zip(levels, blocks):
            share = jnp.exp(level - top)
            total = total + share
            result = result + share * block[:ROWS, :].astype(jnp.float32)
        out[:, h * HD : (h + 1) * HD] = (result / total).astype(jnp.bfloat16)


def join_kernel(q, k, v, out, sems):
    copies = [
        pltpu.make_async_copy(w, out.at[:, i * 2 * HD : (i + 1) * 2 * HD], sems.at[i])
        for i, w in enumerate((q, k, v))
    ]
    for copy in copies:
        copy.start()
    for copy in copies:
        copy.wait()


def spread_kernel(own, partner, out):
    for h in range(CORES):
        for zr, w in enumerate((own, partner)):
            for i in range(3):
                block = w[:, (2 * i + h) * HD : (2 * i + h + 1) * HD]
                for l in range(ZL):
                    out[l * CORES + h, zr, :, i * HD : (i + 1) * HD] = block


def call(kernel, outs, n_scalars, n_arrays, flops, size, scratch=()):
    return pl.pallas_call(
        kernel,
        out_shape=outs,
        in_specs=[SMEM] * n_scalars + [VMEM] * n_arrays,
        out_specs=[VMEM] * len(outs),
        scratch_shapes=list(scratch),
        compiler_params=pltpu.CompilerParams(vmem_limit_bytes=LIMIT),
        cost_estimate=pl.CostEstimate(flops=flops, bytes_accessed=size, transcendentals=0),
    )


def shaped(*shape):
    return jax.ShapeDtypeStruct(shape, jnp.bfloat16)


def local(text, feats, count, proj, gain, q_weight, k_weight, v_weight):
    zh, zl, y = lax.axis_index("zh"), lax.axis_index("zl"), lax.axis_index("y")
    core, section = lax.axis_index("core"), lax.axis_index("section")

    turned = jnp.bitwise_xor(jnp.arange(CHIP_ROWS, dtype=jnp.int32), core * ROWS)
    position = ((zh * ZL + zl) * Y + y) * CHIP_ROWS + turned
    ladder = jnp.arange(HD // 2, dtype=jnp.float32) * 2.0 / HD
    angle = position.astype(jnp.float32)[:, None] * (ROPE_BASE ** (-ladder))[None, :]
    cosine = jnp.cos(angle)
    sine = jnp.sin(angle)
    cosine = jnp.concatenate([cosine, cosine], axis=-1)
    sine = jnp.concatenate([-sine, sine], axis=-1)
    gains = gain.astype(jnp.float32).reshape(SECTIONS, TP, 512)
    gains = jnp.where(section == 0, gains, gains[::-1]).reshape(8, 512)
    feats_b = swap(feats, "section")
    weight = pl.pallas_call(
        join_kernel,
        out_shape=shaped(64, 6 * HD),
        in_specs=[pl.BlockSpec(memory_space=pl.ANY)] * 3,
        out_specs=VMEM,
        scratch_shapes=[pltpu.SemaphoreType.DMA((3,))],
        cost_estimate=pl.CostEstimate(flops=0, bytes_accessed=200000, transcendentals=0),
    )(q_weight, k_weight, v_weight)
    weight_b = swap(weight, "zh")

    weight_b, feats_b = lax.optimization_barrier((weight_b, feats_b))
    (weight,) = call(spread_kernel, [shaped(ZL * CORES, ZH, 64, 3 * HD)], 0, 2, 1000, 1 << 20)(
        weight, weight_b
    )
    weight = lax.all_to_all(weight, ("zl", "core"), 0, 0, tiled=True)

    feats = lax.all_gather(jnp.stack([feats, feats_b]), "tp", axis=0)
    (joined,) = call(join_frames_kernel, [shaped(ROWS, 512)], 1, 3, 2 * ROWS * 1024 * 512, 2 << 20)(
        jnp.stack([section, count[0]]), feats, proj.reshape(8, HD, 512), text
    )

    weight, joined = lax.optimization_barrier((weight, joined))
    weight = lax.all_gather(weight, "y", axis=0)
    joined_b = swap(joined, "section")
    own_a = lax.all_gather(joined, "tp", axis=0)
    own_a, joined_b = lax.optimization_barrier((own_a, joined_b))
    other_a = swap(own_a, "core")
    own_b = gather(joined_b, "tp", TP)
    other_b = swap(own_b, "core")
    queries, kv, lines = pl.pallas_call(
        project_kernel,
        out_shape=[
            shaped(CHIP_ROWS, HD),
            shaped(CHIP_ROWS, 2 * HD),
            shaped(ZL, CHIP_ROWS, 2 * HD),
        ],
        in_specs=[SMEM] + [VMEM] * 4 + [pl.BlockSpec(memory_space=pltpu.HBM)] + [VMEM] * 3,
        out_specs=[VMEM] * 3,
        scratch_shapes=[
            pltpu.VMEM((Y, ZL * CORES, ZH, 64, 3 * HD), jnp.bfloat16),
            pltpu.SemaphoreType.DMA((TP,)),
        ],
        compiler_params=pltpu.CompilerParams(vmem_limit_bytes=LIMIT),
        cost_estimate=pl.CostEstimate(
            flops=2 * CHIP_ROWS * 4096 * 3 * HD, bytes_accessed=6 << 20, transcendentals=0
        ),
    )(
        jnp.bitwise_xor(zh, section).reshape(1),
        own_a,
        own_b,
        other_a,
        other_b,
        pltpu.with_memory_space_constraint(weight, pltpu.HBM),
        gains,
        cosine,
        sine,
    )

    kv_b = swap(kv, "zh")
    kv_a = lax.all_to_all(lines, "zl", 0, 0, tiled=True)
    queries = lax.all_gather(queries, "y", axis=0)
    kv_a, kv_b, queries = lax.optimization_barrier((kv_a, kv_b, queries))
    place = jnp.stack([zh, zl, y, core])
    scores = [pltpu.VMEM((2, ZL, CHIP_ROWS, CHIP_ROWS), jnp.float32)]
    state = [jax.ShapeDtypeStruct((Y, CHIP_ROWS, HD), jnp.float32)] * 2
    flops = 4 * 1024 * 1024 * HD
    parts, levels = call(attend_own_kernel, state, 1, 2, flops, 2 << 20, scores)(
        place, queries, kv_a
    )
    kv_b = gather(kv_b, "zl", ZL)
    (parts,) = call(
        attend_rest_kernel, [shaped(Y * CORES, ROWS + 8, HD)], 1, 4, flops, 2 << 20, scores
    )(place, queries, kv_b, parts, levels)

    parts = lax.all_to_all(parts, ("y", "core"), 0, 0, tiled=True)
    (result,) = call(merge_kernel, [shaped(ROWS, 2 * HD)], 0, 1, 1 << 20, 1 << 20)(parts)
    return result


def solution(mesh):
    fine = Mesh(
        mesh.devices.reshape(ZH, ZL, Y, CORES, SECTIONS, TP),
        ("zh", "zl", "y", "core", "section", "tp"),
    )
    ctx = ("zh", "zl", "y", "core")
    in_specs = (P(ctx, F), P(ctx, F), P(ctx), P(None, F), P(), P(ctx, F), P(ctx, F), P(ctx, F))
    return jax.shard_map(
        local, mesh=fine, in_specs=in_specs, out_specs=P(ctx, F), check_vma=False
    )
```

```python
import math

import jax
import jax.numpy as jnp
from jax import lax
from jax.experimental import pallas as pl
from jax.experimental.pallas import tpu as pltpu
from jax.sharding import Mesh, PartitionSpec as P

HD = 128
ROPE_BASE = 1000000.0
NORM_EPS = 1e-05
MASKED = -1e30

ZH, ZL, Y, CORES, SECTIONS, TP = 2, 4, 4, 2, 2, 4
F = ("section", "tp")
ROWS = 128
CHIP_ROWS = 2 * ROWS
SWAP = [(0, 1), (1, 0)]
VMEM = pl.BlockSpec(memory_space=pltpu.VMEM)
SMEM = pl.BlockSpec(memory_space=pltpu.SMEM)
LIMIT = 40 << 20


def swap(v, axis):
    return lax.ppermute(v, axis, SWAP)


def gather(v, axis, n):
    return lax.all_to_all(jnp.broadcast_to(v[None], (n, *v.shape)), axis, 0, 0, tiled=True)


def join_frames_kernel(pick, feats, proj, text, out):
    vision = jnp.zeros((ROWS, 512), jnp.float32)
    for s in range(SECTIONS):
        first = jnp.bitwise_xor(pick[0], s) * TP
        for t in range(TP):
            vision = vision + jnp.dot(
                feats[t, s], proj[first + t], preferred_element_type=jnp.float32
            )
    row = lax.broadcasted_iota(jnp.int32, (ROWS, 512), 0)
    joined = jnp.where(row < pick[1], vision, text[...].astype(jnp.float32))
    out[...] = joined.astype(jnp.bfloat16)


def project_kernel(
    flip, own_a, own_b, other_a, other_b, stored, gain, cosine, sine, q_out, kv_out, lines_out, weight, sem
):
    copies = [
        pltpu.make_async_copy(
            stored.at[:, :, t * CORES : (t + 1) * CORES],
            weight.at[:, :, t * CORES : (t + 1) * CORES],
            sem.at[t],
        )
        for t in range(TP)
    ]
    for copy in copies:
        copy.start()
    tiles = [(own, other, t) for own, other in ((own_a, other_a), (own_b, other_b)) for t in range(TP)]
    squares = jnp.zeros((CHIP_ROWS, 512), jnp.float32)
    for own, other, t in tiles:
        wide = jnp.concatenate([own[t], other[t]], axis=0).astype(jnp.float32)
        squares = squares + wide * wide
    mean_square = jnp.sum(squares, axis=-1, keepdims=True) * (1.0 / 4096)
    inverse = lax.rsqrt(mean_square + NORM_EPS)
    total = jnp.zeros((CHIP_ROWS, 3 * HD), jnp.float32)
    for i, (own, other, t) in enumerate(tiles):
        if i < TP:
            copies[i].wait()
        half = jnp.bitwise_xor(flip[0], i // TP)
        wide = jnp.concatenate([own[t], other[t]], axis=0).astype(jnp.float32)
        normed = (wide * inverse * gain[i : i + 1, :]).astype(jnp.bfloat16)
        block = jnp.concatenate(
            [weight[y, half, t * CORES + c] for y in range(Y) for c in range(CORES)], axis=0
        )
        total = total + jnp.dot(normed, block, preferred_element_type=jnp.float32)
    q = total[:, :HD]
    k = total[:, HD : 2 * HD]
    cos, sin = cosine[...], sine[...]
    q_out[...] = (q * cos + pltpu.roll(q, HD // 2, 1) * sin).astype(jnp.bfloat16)
    k = (k * cos + pltpu.roll(k, HD // 2, 1) * sin).astype(jnp.bfloat16)
    v = total[:, 2 * HD :].astype(jnp.bfloat16)
    kv_out[:, :HD] = k
    kv_out[:, HD:] = v
    for i in range(ZL):
        lines_out[i, :, :HD] = k
        lines_out[i, :, HD:] = v


def encode(level):
    lane = lax.broadcasted_iota(jnp.int32, (CHIP_ROWS, HD), 1)
    high = level.astype(jnp.bfloat16).astype(jnp.float32)
    rest = level - high
    middle = rest.astype(jnp.bfloat16).astype(jnp.float32)
    low = rest - middle
    coded = jnp.where(
        lane == 0, high, jnp.where(lane == 1, middle, jnp.where(lane == 2, low, 0.0))
    ).astype(jnp.bfloat16)
    pick = lax.broadcasted_iota(jnp.int32, (8, HD), 0) == lax.broadcasted_iota(jnp.int32, (8, HD), 1)
    pick = pick.astype(jnp.float32).astype(jnp.bfloat16)
    coded = lax.dot_general(
        pick, coded, (((1,), (1,)), ((), ())), preferred_element_type=jnp.float32
    )
    return jnp.concatenate([coded[:, :ROWS], coded[:, ROWS:]], axis=0).astype(jnp.bfloat16)


def decode(coded):
    shape = (ROWS, ROWS)
    eye = lax.broadcasted_iota(jnp.int32, shape, 0) == lax.broadcasted_iota(jnp.int32, shape, 1)
    eye = eye.astype(jnp.float32).astype(jnp.bfloat16)
    c = lax.dot_general(eye, coded, (((1,), (1,)), ((), ())), preferred_element_type=jnp.float32)
    return c[:, 0:1] + c[:, 1:2] + c[:, 2:3]


def attend(q, kv, scores, mask):
    shape = (CHIP_ROWS, CHIP_ROWS)
    scale = 1.0 / math.sqrt(HD)
    peak = jnp.full(shape, MASKED, jnp.float32)
    for l in range(ZL):
        s = lax.dot_general(
            q, kv[l, :, :HD], (((1,), (1,)), ((), ())), preferred_element_type=jnp.float32
        )
        s = mask(l, s * scale)
        scores[l] = s
        peak = jnp.maximum(peak, s)
    best = jnp.max(peak, axis=-1, keepdims=True)
    mass = jnp.zeros(shape, jnp.float32)
    part = jnp.zeros((CHIP_ROWS, HD), jnp.float32)
    for l in range(ZL):
        w = jnp.exp(scores[l] - best)
        mass = mass + w
        part = part + jnp.dot(
            w.astype(jnp.bfloat16), kv[l, :, HD:], preferred_element_type=jnp.float32
        )
    total = jnp.sum(mass, axis=-1, keepdims=True)
    return part / total, jnp.where(best > 0.5 * MASKED, best + jnp.log(total), MASKED)


def attend_own_kernel(place, queries, kv, parts, levels, scores):
    zl, me, core = place[1], place[2], place[3]
    shape = (CHIP_ROWS, CHIP_ROWS)
    turn = core * ROWS
    row = jnp.bitwise_xor(lax.broadcasted_iota(jnp.int32, shape, 0), turn)
    col = jnp.bitwise_xor(lax.broadcasted_iota(jnp.int32, shape, 1), turn)
    ahead = col - row

    def one(pair, carry):
        for i in range(2):
            y = pair * 2 + i

            def mask(l, s):
                return jnp.where(ahead <= ((zl - l) * Y + y - me) * CHIP_ROWS, s, MASKED)

            part, level = attend(queries[y], kv, scores.at[i], mask)
            parts[y] = part
            levels[y] = jnp.broadcast_to(level, (CHIP_ROWS, HD))
        return carry

    lax.fori_loop(0, Y // 2, one, 0)


def attend_rest_kernel(place, queries, kv, parts, levels, out, scores):
    def put(y, part, level):
        coded = encode(level)
        part = part.astype(jnp.bfloat16)
        for i in range(CORES):
            owner = y * CORES + jnp.bitwise_xor(place[3], i)
            out[owner, :ROWS, :] = part[i * ROWS : (i + 1) * ROWS]
            out[owner, ROWS:, :] = coded[i * 8 : (i + 1) * 8]

    @pl.when(place[0] == 0)
    def _():
        for y in range(Y):
            put(y, parts[y], levels[y, :, 0:1])

    @pl.when(place[0] != 0)
    def _():
        def one(pair, carry):
            for i in range(2):
                y = pair * 2 + i
                part, level = attend(queries[y], kv, scores.at[i], lambda l, s: s)
                before = levels[y, :, 0:1]
                top = jnp.maximum(level, before)
                new, old = jnp.exp(level - top), jnp.exp(before - top)
                total = new + old
                put(y, (part * new + parts[y] * old) / total, top + jnp.log(total))
            return carry

        lax.fori_loop(0, Y // 2, one, 0)


def merge_kernel(parts, out):
    for h in range(CORES):
        blocks = [parts[y * CORES + h] for y in range(Y)]
        levels = [decode(block[ROWS:, :]) for block in blocks]
        top = jnp.maximum(jnp.maximum(levels[0], levels[1]), jnp.maximum(levels[2], levels[3]))
        total = jnp.zeros_like(top)
        result = jnp.zeros((ROWS, HD), jnp.float32)
        for level, block in zip(levels, blocks):
            share = jnp.exp(level - top)
            total = total + share
            result = result + share * block[:ROWS, :].astype(jnp.float32)
        out[:, h * HD : (h + 1) * HD] = (result / total).astype(jnp.bfloat16)


def spread_kernel(w, out):
    for h in range(CORES):
        for i in range(3):
            block = w[:, (2 * i + h) * HD : (2 * i + h + 1) * HD]
            for l in range(ZL):
                out[l * CORES + h, :, i * HD : (i + 1) * HD] = block


def join_kernel(q, k, v, joined, out, sems):
    copies = [
        pltpu.make_async_copy(w, joined.at[:, i * 2 * HD : (i + 1) * 2 * HD], sems.at[i])
        for i, w in enumerate((q, k, v))
    ]
    for copy in copies:
        copy.start()
    for copy in copies:
        copy.wait()
    spread_kernel(joined, out)


def call(kernel, outs, n_scalars, n_arrays, flops, size, scratch=()):
    return pl.pallas_call(
        kernel,
        out_shape=outs,
        in_specs=[SMEM] * n_scalars + [VMEM] * n_arrays,
        out_specs=[VMEM] * len(outs),
        scratch_shapes=list(scratch),
        compiler_params=pltpu.CompilerParams(vmem_limit_bytes=LIMIT),
        cost_estimate=pl.CostEstimate(flops=flops, bytes_accessed=size, transcendentals=0),
    )


def shaped(*shape):
    return jax.ShapeDtypeStruct(shape, jnp.bfloat16)


def local(text, feats, count, proj, gain, q_weight, k_weight, v_weight):
    zh, zl, y = lax.axis_index("zh"), lax.axis_index("zl"), lax.axis_index("y")
    core, section = lax.axis_index("core"), lax.axis_index("section")

    turned = jnp.bitwise_xor(jnp.arange(CHIP_ROWS, dtype=jnp.int32), core * ROWS)
    position = ((zh * ZL + zl) * Y + y) * CHIP_ROWS + turned
    ladder = jnp.arange(HD // 2, dtype=jnp.float32) * 2.0 / HD
    angle = position.astype(jnp.float32)[:, None] * (ROPE_BASE ** (-ladder))[None, :]
    cosine = jnp.cos(angle)
    sine = jnp.sin(angle)
    cosine = jnp.concatenate([cosine, cosine], axis=-1)
    sine = jnp.concatenate([-sine, sine], axis=-1)
    gains = gain.astype(jnp.float32).reshape(SECTIONS, TP, 512)
    gains = jnp.where(section == 0, gains, gains[::-1]).reshape(8, 512)
    feats_b = swap(feats, "section")
    weight, spread = pl.pallas_call(
        join_kernel,
        out_shape=[shaped(64, 6 * HD), shaped(ZL * CORES, 64, 3 * HD)],
        in_specs=[pl.BlockSpec(memory_space=pl.ANY)] * 3,
        out_specs=[VMEM] * 2,
        scratch_shapes=[pltpu.SemaphoreType.DMA((3,))],
        cost_estimate=pl.CostEstimate(flops=0, bytes_accessed=800000, transcendentals=0),
    )(q_weight, k_weight, v_weight)
    weight_b = swap(weight, "zh")
    weight_a = lax.all_to_all(spread, ("zl", "core"), 0, 0, tiled=True)
    weight_a, weight_b, feats_b = lax.optimization_barrier((weight_a, weight_b, feats_b))
    (spread,) = call(spread_kernel, [shaped(ZL * CORES, 64, 3 * HD)], 0, 1, 1000, 1 << 20)(weight_b)
    weight_b = lax.all_to_all(spread, ("zl", "core"), 0, 0, tiled=True)

    feats = lax.all_gather(jnp.stack([feats, feats_b]), "tp", axis=0)
    (joined,) = call(join_frames_kernel, [shaped(ROWS, 512)], 1, 3, 2 * ROWS * 1024 * 512, 2 << 20)(
        jnp.stack([section, count[0]]), feats, proj.reshape(8, HD, 512), text
    )

    weight_b, joined = lax.optimization_barrier((weight_b, joined))
    weight = lax.all_gather(jnp.stack([weight_a, weight_b]), "y", axis=0)
    joined_b = swap(joined, "section")
    own_a = lax.all_gather(joined, "tp", axis=0)
    own_a, joined_b = lax.optimization_barrier((own_a, joined_b))
    other_a = swap(own_a, "core")
    own_b = gather(joined_b, "tp", TP)
    other_b = swap(own_b, "core")
    queries, kv, lines = pl.pallas_call(
        project_kernel,
        out_shape=[
            shaped(CHIP_ROWS, HD),
            shaped(CHIP_ROWS, 2 * HD),
            shaped(ZL, CHIP_ROWS, 2 * HD),
        ],
        in_specs=[SMEM] + [VMEM] * 4 + [pl.BlockSpec(memory_space=pltpu.HBM)] + [VMEM] * 3,
        out_specs=[VMEM] * 3,
        scratch_shapes=[
            pltpu.VMEM((Y, ZH, ZL * CORES, 64, 3 * HD), jnp.bfloat16),
            pltpu.SemaphoreType.DMA((TP,)),
        ],
        compiler_params=pltpu.CompilerParams(vmem_limit_bytes=LIMIT),
        cost_estimate=pl.CostEstimate(
            flops=2 * CHIP_ROWS * 4096 * 3 * HD, bytes_accessed=6 << 20, transcendentals=0
        ),
    )(
        jnp.bitwise_xor(zh, section).reshape(1),
        own_a,
        own_b,
        other_a,
        other_b,
        pltpu.with_memory_space_constraint(weight, pltpu.HBM),
        gains,
        cosine,
        sine,
    )

    kv_b = swap(kv, "zh")
    kv_a = lax.all_to_all(lines, "zl", 0, 0, tiled=True)
    queries = lax.all_gather(queries, "y", axis=0)
    kv_a, kv_b, queries = lax.optimization_barrier((kv_a, kv_b, queries))
    place = jnp.stack([zh, zl, y, core])
    scores = [pltpu.VMEM((2, ZL, CHIP_ROWS, CHIP_ROWS), jnp.float32)]
    state = [jax.ShapeDtypeStruct((Y, CHIP_ROWS, HD), jnp.float32)] * 2
    flops = 4 * 1024 * 1024 * HD
    parts, levels = call(attend_own_kernel, state, 1, 2, flops, 2 << 20, scores)(
        place, queries, kv_a
    )
    kv_b = gather(kv_b, "zl", ZL)
    (parts,) = call(
        attend_rest_kernel, [shaped(Y * CORES, ROWS + 8, HD)], 1, 4, flops, 2 << 20, scores
    )(place, queries, kv_b, parts, levels)

    parts = lax.all_to_all(parts, ("y", "core"), 0, 0, tiled=True)
    (result,) = call(merge_kernel, [shaped(ROWS, 2 * HD)], 0, 1, 1 << 20, 1 << 20)(parts)
    return result


def solution(mesh):
    fine = Mesh(
        mesh.devices.reshape(ZH, ZL, Y, CORES, SECTIONS, TP),
        ("zh", "zl", "y", "core", "section", "tp"),
    )
    ctx = ("zh", "zl", "y", "core")
    in_specs = (P(ctx, F), P(ctx, F), P(ctx), P(None, F), P(), P(ctx, F), P(ctx, F), P(ctx, F))
    return jax.shard_map(
        local, mesh=fine, in_specs=in_specs, out_specs=P(ctx, F), check_vma=False
    )
```

```python
import math

import jax
import jax.numpy as jnp
from jax import lax
from jax.experimental import pallas as pl
from jax.experimental.pallas import tpu as pltpu
from jax.sharding import Mesh, PartitionSpec as P

HD = 128
ROPE_BASE = 1000000.0
NORM_EPS = 1e-05
MASKED = -1e30

ZH, ZL, Y, CORES, SECTIONS, TP = 2, 4, 4, 2, 2, 4
F = ("section", "tp")
ROWS = 128
CHIP_ROWS = 2 * ROWS
SWAP = [(0, 1), (1, 0)]
VMEM = pl.BlockSpec(memory_space=pltpu.VMEM)
SMEM = pl.BlockSpec(memory_space=pltpu.SMEM)
LIMIT = 40 << 20


def swap(v, axis):
    return lax.ppermute(v, axis, SWAP)


def gather(v, axis, n):
    return lax.all_to_all(jnp.broadcast_to(v[None], (n, *v.shape)), axis, 0, 0, tiled=True)


def join_frames_kernel(pick, feats, proj, text, out):
    vision = jnp.zeros((ROWS, 512), jnp.float32)
    for s in range(SECTIONS):
        first = jnp.bitwise_xor(pick[0], s) * TP
        for t in range(TP):
            vision = vision + jnp.dot(
                feats[t, s], proj[first + t], preferred_element_type=jnp.float32
            )
    row = lax.broadcasted_iota(jnp.int32, (ROWS, 512), 0)
    joined = jnp.where(row < pick[1], vision, text[...].astype(jnp.float32))
    out[...] = joined.astype(jnp.bfloat16)


def project_kernel(
    flip, own_a, own_b, other_a, other_b, stored, gain, cosine, sine, q_out, kv_out, lines_out, weight, sem
):
    copies = [
        pltpu.make_async_copy(
            stored.at[:, :, t * CORES : (t + 1) * CORES],
            weight.at[:, :, t * CORES : (t + 1) * CORES],
            sem.at[t],
        )
        for t in range(TP)
    ]
    for copy in copies:
        copy.start()
    tiles = [(own, other, t) for own, other in ((own_a, other_a), (own_b, other_b)) for t in range(TP)]
    squares = jnp.zeros((CHIP_ROWS, 512), jnp.float32)
    for own, other, t in tiles:
        wide = jnp.concatenate([own[t], other[t]], axis=0).astype(jnp.float32)
        squares = squares + wide * wide
    mean_square = jnp.sum(squares, axis=-1, keepdims=True) * (1.0 / 4096)
    inverse = lax.rsqrt(mean_square + NORM_EPS)
    total = jnp.zeros((CHIP_ROWS, 3 * HD), jnp.float32)
    for i, (own, other, t) in enumerate(tiles):
        if i < TP:
            copies[i].wait()
        half = jnp.bitwise_xor(flip[0], i // TP)
        wide = jnp.concatenate([own[t], other[t]], axis=0).astype(jnp.float32)
        normed = (wide * inverse * gain[i : i + 1, :]).astype(jnp.bfloat16)
        block = jnp.concatenate(
            [weight[y, half, t * CORES + c] for y in range(Y) for c in range(CORES)], axis=0
        )
        total = total + jnp.dot(normed, block, preferred_element_type=jnp.float32)
    q = total[:, :HD]
    k = total[:, HD : 2 * HD]
    cos, sin = cosine[...], sine[...]
    q_out[...] = (q * cos + pltpu.roll(q, HD // 2, 1) * sin).astype(jnp.bfloat16)
    k = (k * cos + pltpu.roll(k, HD // 2, 1) * sin).astype(jnp.bfloat16)
    v = total[:, 2 * HD :].astype(jnp.bfloat16)
    kv_out[:, :HD] = k
    kv_out[:, HD:] = v
    for i in range(ZL):
        lines_out[i, :, :HD] = k
        lines_out[i, :, HD:] = v


def encode(level):
    lane = lax.broadcasted_iota(jnp.int32, (CHIP_ROWS, HD), 1)
    high = level.astype(jnp.bfloat16).astype(jnp.float32)
    rest = level - high
    middle = rest.astype(jnp.bfloat16).astype(jnp.float32)
    low = rest - middle
    coded = jnp.where(
        lane == 0, high, jnp.where(lane == 1, middle, jnp.where(lane == 2, low, 0.0))
    ).astype(jnp.bfloat16)
    pick = lax.broadcasted_iota(jnp.int32, (8, HD), 0) == lax.broadcasted_iota(jnp.int32, (8, HD), 1)
    pick = pick.astype(jnp.float32).astype(jnp.bfloat16)
    coded = lax.dot_general(
        pick, coded, (((1,), (1,)), ((), ())), preferred_element_type=jnp.float32
    )
    return jnp.concatenate([coded[:, :ROWS], coded[:, ROWS:]], axis=0).astype(jnp.bfloat16)


def decode(coded):
    shape = (ROWS, ROWS)
    eye = lax.broadcasted_iota(jnp.int32, shape, 0) == lax.broadcasted_iota(jnp.int32, shape, 1)
    eye = eye.astype(jnp.float32).astype(jnp.bfloat16)
    c = lax.dot_general(eye, coded, (((1,), (1,)), ((), ())), preferred_element_type=jnp.float32)
    return c[:, 0:1] + c[:, 1:2] + c[:, 2:3]


def attend(q, kv, scores, mask):
    shape = (CHIP_ROWS, CHIP_ROWS)
    scale = 1.0 / math.sqrt(HD)
    peak = jnp.full(shape, MASKED, jnp.float32)
    for l in range(ZL):
        s = lax.dot_general(
            q, kv[l, :, :HD], (((1,), (1,)), ((), ())), preferred_element_type=jnp.float32
        )
        s = mask(l, s * scale)
        scores[l] = s
        peak = jnp.maximum(peak, s)
    best = jnp.max(peak, axis=-1, keepdims=True)
    mass = jnp.zeros(shape, jnp.float32)
    part = jnp.zeros((CHIP_ROWS, HD), jnp.float32)
    for l in range(ZL):
        w = jnp.exp(scores[l] - best)
        mass = mass + w
        part = part + jnp.dot(
            w.astype(jnp.bfloat16), kv[l, :, HD:], preferred_element_type=jnp.float32
        )
    total = jnp.sum(mass, axis=-1, keepdims=True)
    return part / total, jnp.where(best > 0.5 * MASKED, best + jnp.log(total), MASKED)


def attend_own_kernel(place, queries, kv, parts, levels, scores):
    zl, me, core = place[1], place[2], place[3]
    shape = (CHIP_ROWS, CHIP_ROWS)
    turn = core * ROWS
    row = jnp.bitwise_xor(lax.broadcasted_iota(jnp.int32, shape, 0), turn)
    col = jnp.bitwise_xor(lax.broadcasted_iota(jnp.int32, shape, 1), turn)
    ahead = col - row

    def one(pair, carry):
        for i in range(2):
            y = pair * 2 + i

            def mask(l, s):
                return jnp.where(ahead <= ((zl - l) * Y + y - me) * CHIP_ROWS, s, MASKED)

            part, level = attend(queries[y], kv, scores.at[i], mask)
            parts[y] = part
            levels[y] = jnp.broadcast_to(level, (CHIP_ROWS, HD))
        return carry

    lax.fori_loop(0, Y // 2, one, 0)


def attend_rest_kernel(place, queries, kv, parts, levels, out, scores):
    def put(y, part, level):
        coded = encode(level)
        part = part.astype(jnp.bfloat16)
        for i in range(CORES):
            owner = y * CORES + jnp.bitwise_xor(place[3], i)
            out[owner, :ROWS, :] = part[i * ROWS : (i + 1) * ROWS]
            out[owner, ROWS:, :] = coded[i * 8 : (i + 1) * 8]

    @pl.when(place[0] == 0)
    def _():
        for y in range(Y):
            put(y, parts[y], levels[y, :, 0:1])

    @pl.when(place[0] != 0)
    def _():
        def one(pair, carry):
            for i in range(2):
                y = pair * 2 + i
                part, level = attend(queries[y], kv, scores.at[i], lambda l, s: s)
                before = levels[y, :, 0:1]
                top = jnp.maximum(level, before)
                new, old = jnp.exp(level - top), jnp.exp(before - top)
                total = new + old
                put(y, (part * new + parts[y] * old) / total, top + jnp.log(total))
            return carry

        lax.fori_loop(0, Y // 2, one, 0)


def merge_kernel(parts, out):
    for h in range(CORES):
        blocks = [parts[y * CORES + h] for y in range(Y)]
        levels = [decode(block[ROWS:, :]) for block in blocks]
        top = jnp.maximum(jnp.maximum(levels[0], levels[1]), jnp.maximum(levels[2], levels[3]))
        total = jnp.zeros_like(top)
        result = jnp.zeros((ROWS, HD), jnp.float32)
        for level, block in zip(levels, blocks):
            share = jnp.exp(level - top)
            total = total + share
            result = result + share * block[:ROWS, :].astype(jnp.float32)
        out[:, h * HD : (h + 1) * HD] = (result / total).astype(jnp.bfloat16)


def spread_kernel(w, out):
    for h in range(CORES):
        for i in range(3):
            block = w[:, (2 * i + h) * HD : (2 * i + h + 1) * HD]
            for l in range(ZL):
                out[l * CORES + h, :, i * HD : (i + 1) * HD] = block


def join_kernel(q, k, v, joined, out, sems):
    copies = [
        pltpu.make_async_copy(w, joined.at[:, i * 2 * HD : (i + 1) * 2 * HD], sems.at[i])
        for i, w in enumerate((q, k, v))
    ]
    for copy in copies:
        copy.start()
    for copy in copies:
        copy.wait()
    spread_kernel(joined, out)


def call(kernel, outs, n_scalars, n_arrays, flops, size, scratch=()):
    return pl.pallas_call(
        kernel,
        out_shape=outs,
        in_specs=[SMEM] * n_scalars + [VMEM] * n_arrays,
        out_specs=[VMEM] * len(outs),
        scratch_shapes=list(scratch),
        compiler_params=pltpu.CompilerParams(vmem_limit_bytes=LIMIT),
        cost_estimate=pl.CostEstimate(flops=flops, bytes_accessed=size, transcendentals=0),
    )


def shaped(*shape):
    return jax.ShapeDtypeStruct(shape, jnp.bfloat16)


def local(text, feats, count, proj, gain, q_weight, k_weight, v_weight):
    zh, zl, y = lax.axis_index("zh"), lax.axis_index("zl"), lax.axis_index("y")
    core, section = lax.axis_index("core"), lax.axis_index("section")

    turned = jnp.bitwise_xor(jnp.arange(CHIP_ROWS, dtype=jnp.int32), core * ROWS)
    position = ((zh * ZL + zl) * Y + y) * CHIP_ROWS + turned
    ladder = jnp.arange(HD // 2, dtype=jnp.float32) * 2.0 / HD
    angle = position.astype(jnp.float32)[:, None] * (ROPE_BASE ** (-ladder))[None, :]
    cosine = jnp.cos(angle)
    sine = jnp.sin(angle)
    cosine = jnp.concatenate([cosine, cosine], axis=-1)
    sine = jnp.concatenate([-sine, sine], axis=-1)
    gains = gain.astype(jnp.float32).reshape(SECTIONS, TP, 512)
    gains = jnp.where(section == 0, gains, gains[::-1]).reshape(8, 512)
    feats_b = swap(feats, "section")
    weight, spread = pl.pallas_call(
        join_kernel,
        out_shape=[shaped(64, 6 * HD), shaped(ZL * CORES, 64, 3 * HD)],
        in_specs=[pl.BlockSpec(memory_space=pl.ANY)] * 3,
        out_specs=[VMEM] * 2,
        scratch_shapes=[pltpu.SemaphoreType.DMA((3,))],
        cost_estimate=pl.CostEstimate(flops=0, bytes_accessed=800000, transcendentals=0),
    )(q_weight, k_weight, v_weight)
    weight_b = swap(weight, "zh")
    weight_a = lax.all_to_all(spread, ("zl", "core"), 0, 0, tiled=True)
    feats = lax.all_gather(jnp.stack([feats, feats_b]), "tp", axis=0)
    (joined,) = call(join_frames_kernel, [shaped(ROWS, 512)], 1, 3, 2 * ROWS * 1024 * 512, 2 << 20)(
        jnp.stack([section, count[0]]), feats, proj.reshape(8, HD, 512), text
    )

    weight_a, weight_b, joined = lax.optimization_barrier((weight_a, weight_b, joined))
    (spread,) = call(spread_kernel, [shaped(ZL * CORES, 64, 3 * HD)], 0, 1, 1000, 1 << 20)(weight_b)
    weight_b = lax.all_to_all(spread, ("zl", "core"), 0, 0, tiled=True)
    weight = lax.all_gather(jnp.stack([weight_a, weight_b]), "y", axis=0)
    joined_b = swap(joined, "section")
    own_a = lax.all_gather(joined, "tp", axis=0)
    own_a, joined_b = lax.optimization_barrier((own_a, joined_b))
    other_a = swap(own_a, "core")
    own_b = gather(joined_b, "tp", TP)
    other_b = swap(own_b, "core")
    queries, kv, lines = pl.pallas_call(
        project_kernel,
        out_shape=[
            shaped(CHIP_ROWS, HD),
            shaped(CHIP_ROWS, 2 * HD),
            shaped(ZL, CHIP_ROWS, 2 * HD),
        ],
        in_specs=[SMEM] + [VMEM] * 4 + [pl.BlockSpec(memory_space=pltpu.HBM)] + [VMEM] * 3,
        out_specs=[VMEM] * 3,
        scratch_shapes=[
            pltpu.VMEM((Y, ZH, ZL * CORES, 64, 3 * HD), jnp.bfloat16),
            pltpu.SemaphoreType.DMA((TP,)),
        ],
        compiler_params=pltpu.CompilerParams(vmem_limit_bytes=LIMIT),
        cost_estimate=pl.CostEstimate(
            flops=2 * CHIP_ROWS * 4096 * 3 * HD, bytes_accessed=6 << 20, transcendentals=0
        ),
    )(
        jnp.bitwise_xor(zh, section).reshape(1),
        own_a,
        own_b,
        other_a,
        other_b,
        pltpu.with_memory_space_constraint(weight, pltpu.HBM),
        gains,
        cosine,
        sine,
    )

    kv_b = swap(kv, "zh")
    kv_a = lax.all_to_all(lines, "zl", 0, 0, tiled=True)
    queries = lax.all_gather(queries, "y", axis=0)
    kv_a, kv_b, queries = lax.optimization_barrier((kv_a, kv_b, queries))
    place = jnp.stack([zh, zl, y, core])
    scores = [pltpu.VMEM((2, ZL, CHIP_ROWS, CHIP_ROWS), jnp.float32)]
    state = [jax.ShapeDtypeStruct((Y, CHIP_ROWS, HD), jnp.float32)] * 2
    flops = 4 * 1024 * 1024 * HD
    parts, levels = call(attend_own_kernel, state, 1, 2, flops, 2 << 20, scores)(
        place, queries, kv_a
    )
    kv_b = gather(kv_b, "zl", ZL)
    (parts,) = call(
        attend_rest_kernel, [shaped(Y * CORES, ROWS + 8, HD)], 1, 4, flops, 2 << 20, scores
    )(place, queries, kv_b, parts, levels)

    parts = lax.all_to_all(parts, ("y", "core"), 0, 0, tiled=True)
    (result,) = call(merge_kernel, [shaped(ROWS, 2 * HD)], 0, 1, 1 << 20, 1 << 20)(parts)
    return result


def solution(mesh):
    fine = Mesh(
        mesh.devices.reshape(ZH, ZL, Y, CORES, SECTIONS, TP),
        ("zh", "zl", "y", "core", "section", "tp"),
    )
    ctx = ("zh", "zl", "y", "core")
    in_specs = (P(ctx, F), P(ctx, F), P(ctx), P(None, F), P(), P(ctx, F), P(ctx, F), P(ctx, F))
    return jax.shard_map(
        local, mesh=fine, in_specs=in_specs, out_specs=P(ctx, F), check_vma=False
    )
```

```python
import math

import jax
import jax.numpy as jnp
from jax import lax
from jax.experimental import pallas as pl
from jax.experimental.pallas import tpu as pltpu
from jax.sharding import Mesh, PartitionSpec as P

HD = 128
ROPE_BASE = 1000000.0
NORM_EPS = 1e-05
MASKED = -1e30

ZH, ZL, Y, CORES, SECTIONS, TP = 2, 4, 4, 2, 2, 4
F = ("section", "tp")
ROWS = 128
CHIP_ROWS = 2 * ROWS
SWAP = [(0, 1), (1, 0)]
VMEM = pl.BlockSpec(memory_space=pltpu.VMEM)
SMEM = pl.BlockSpec(memory_space=pltpu.SMEM)
LIMIT = 40 << 20


def swap(v, axis):
    return lax.ppermute(v, axis, SWAP)


def gather(v, axis, n):
    return lax.all_to_all(jnp.broadcast_to(v[None], (n, *v.shape)), axis, 0, 0, tiled=True)


def join_frames_kernel(pick, feats, proj, text, out):
    vision = jnp.zeros((ROWS, 512), jnp.float32)
    for s in range(SECTIONS):
        first = jnp.bitwise_xor(pick[0], s) * TP
        for t in range(TP):
            vision = vision + jnp.dot(
                feats[t, s], proj[first + t], preferred_element_type=jnp.float32
            )
    row = lax.broadcasted_iota(jnp.int32, (ROWS, 512), 0)
    joined = jnp.where(row < pick[1], vision, text[...].astype(jnp.float32))
    out[...] = joined.astype(jnp.bfloat16)


def project_kernel(
    flip, own_a, own_b, other_a, other_b, stored, gain, cosine, sine, q_out, kv_out, lines_out, weight, sem
):
    copies = [
        pltpu.make_async_copy(
            stored.at[:, t * CORES : (t + 1) * CORES], weight.at[:, t * CORES : (t + 1) * CORES], sem.at[t]
        )
        for t in range(TP)
    ]
    for copy in copies:
        copy.start()
    tiles = [(own, other, t) for own, other in ((own_a, other_a), (own_b, other_b)) for t in range(TP)]
    squares = jnp.zeros((CHIP_ROWS, 512), jnp.float32)
    for own, other, t in tiles:
        wide = jnp.concatenate([own[t], other[t]], axis=0).astype(jnp.float32)
        squares = squares + wide * wide
    mean_square = jnp.sum(squares, axis=-1, keepdims=True) * (1.0 / 4096)
    inverse = lax.rsqrt(mean_square + NORM_EPS)
    total = jnp.zeros((CHIP_ROWS, 3 * HD), jnp.float32)
    for i, (own, other, t) in enumerate(tiles):
        if i < TP:
            copies[i].wait()
        half = jnp.bitwise_xor(flip[0], i // TP)
        wide = jnp.concatenate([own[t], other[t]], axis=0).astype(jnp.float32)
        normed = (wide * inverse * gain[i : i + 1, :]).astype(jnp.bfloat16)
        block = jnp.concatenate(
            [weight[y, t * CORES + c, half] for y in range(Y) for c in range(CORES)], axis=0
        )
        total = total + jnp.dot(normed, block, preferred_element_type=jnp.float32)
    q = total[:, :HD]
    k = total[:, HD : 2 * HD]
    cos, sin = cosine[...], sine[...]
    q_out[...] = (q * cos + pltpu.roll(q, HD // 2, 1) * sin).astype(jnp.bfloat16)
    k = (k * cos + pltpu.roll(k, HD // 2, 1) * sin).astype(jnp.bfloat16)
    v = total[:, 2 * HD :].astype(jnp.bfloat16)
    kv_out[:, :HD] = k
    kv_out[:, HD:] = v
    for i in range(ZL):
        lines_out[i, :, :HD] = k
        lines_out[i, :, HD:] = v


def encode(level):
    lane = lax.broadcasted_iota(jnp.int32, (CHIP_ROWS, HD), 1)
    high = level.astype(jnp.bfloat16).astype(jnp.float32)
    rest = level - high
    middle = rest.astype(jnp.bfloat16).astype(jnp.float32)
    low = rest - middle
    coded = jnp.where(
        lane == 0, high, jnp.where(lane == 1, middle, jnp.where(lane == 2, low, 0.0))
    ).astype(jnp.bfloat16)
    pick = lax.broadcasted_iota(jnp.int32, (8, HD), 0) == lax.broadcasted_iota(jnp.int32, (8, HD), 1)
    pick = pick.astype(jnp.float32).astype(jnp.bfloat16)
    coded = lax.dot_general(
        pick, coded, (((1,), (1,)), ((), ())), preferred_element_type=jnp.float32
    )
    return jnp.concatenate([coded[:, :ROWS], coded[:, ROWS:]], axis=0).astype(jnp.bfloat16)


def attend(q, kv, scores, mask):
    shape = (CHIP_ROWS, CHIP_ROWS)
    scale = 1.0 / math.sqrt(HD)
    peak = jnp.full(shape, MASKED, jnp.float32)
    for l in range(ZL):
        s = lax.dot_general(
            q, kv[l, :, :HD], (((1,), (1,)), ((), ())), preferred_element_type=jnp.float32
        )
        s = mask(l, s * scale)
        scores[l] = s
        peak = jnp.maximum(peak, s)
    best = jnp.max(peak, axis=-1, keepdims=True)
    mass = jnp.zeros(shape, jnp.float32)
    part = jnp.zeros((CHIP_ROWS, HD), jnp.float32)
    for l in range(ZL):
        w = jnp.exp(scores[l] - best)
        mass = mass + w
        part = part + jnp.dot(
            w.astype(jnp.bfloat16), kv[l, :, HD:], preferred_element_type=jnp.float32
        )
    total = jnp.sum(mass, axis=-1, keepdims=True)
    return part / total, jnp.where(best > 0.5 * MASKED, best + jnp.log(total), MASKED)


def attend_own_kernel(place, queries, kv, parts, levels, scores):
    zl, me, core = place[1], place[2], place[3]
    shape = (CHIP_ROWS, CHIP_ROWS)
    turn = core * ROWS
    row = jnp.bitwise_xor(lax.broadcasted_iota(jnp.int32, shape, 0), turn)
    col = jnp.bitwise_xor(lax.broadcasted_iota(jnp.int32, shape, 1), turn)
    ahead = col - row

    def one(pair, carry):
        for i in range(2):
            y = pair * 2 + i

            def mask(l, s):
                return jnp.where(ahead <= ((zl - l) * Y + y - me) * CHIP_ROWS, s, MASKED)

            part, level = attend(queries[y], kv, scores.at[i], mask)
            parts[y] = part
            levels[y] = jnp.broadcast_to(level, (CHIP_ROWS, HD))
        return carry

    lax.fori_loop(0, Y // 2, one, 0)


def attend_rest_kernel(place, queries, kv, parts, levels, out, scores):
    def put(y, part, level):
        coded = encode(level)
        part = part.astype(jnp.bfloat16)
        for i in range(CORES):
            owner = y * CORES + jnp.bitwise_xor(place[3], i)
            out[owner, :ROWS, :] = part[i * ROWS : (i + 1) * ROWS]
            out[owner, ROWS:, :] = coded[i * 8 : (i + 1) * 8]

    @pl.when(place[0] == 0)
    def _():
        for y in range(Y):
            put(y, parts[y], levels[y, :, 0:1])

    @pl.when(place[0] != 0)
    def _():
        for y in range(Y):
            part, level = attend(queries[y], kv, scores.at[y], lambda l, s: s)
            before = levels[y, :, 0:1]
            top = jnp.maximum(level, before)
            new, old = jnp.exp(level - top), jnp.exp(before - top)
            total = new + old
            put(y, (part * new + parts[y] * old) / total, top + jnp.log(total))


def merge_kernel(parts, out):
    shares = []
    for h in range(CORES):
        levels = []
        for y in range(Y):
            coded = parts[y * CORES + h, ROWS:, :].astype(jnp.float32)
            levels.append(coded[0:1] + coded[1:2] + coded[2:3])
        levels = jnp.concatenate(levels, axis=0)
        share = jnp.exp(levels - jnp.max(levels, axis=0, keepdims=True))
        shares.append(share / jnp.sum(share, axis=0, keepdims=True))
    shares = jnp.transpose(jnp.concatenate(shares * (ROWS // (CORES * Y)), axis=0))
    for h in range(CORES):
        result = jnp.zeros((ROWS, HD), jnp.float32)
        for y in range(Y):
            lane = h * Y + y
            block = parts[y * CORES + h, :ROWS, :].astype(jnp.float32)
            result = result + shares[:, lane : lane + 1] * block
        out[:, h * HD : (h + 1) * HD] = result.astype(jnp.bfloat16)


def join_kernel(q, k, v, out, sems):
    copies = [
        pltpu.make_async_copy(w, out.at[:, i * 2 * HD : (i + 1) * 2 * HD], sems.at[i])
        for i, w in enumerate((q, k, v))
    ]
    for copy in copies:
        copy.start()
    for copy in copies:
        copy.wait()


def spread_kernel(own, partner, out):
    for h in range(CORES):
        for zr, w in enumerate((own, partner)):
            for i in range(3):
                block = w[:, (2 * i + h) * HD : (2 * i + h + 1) * HD]
                for l in range(ZL):
                    out[l * CORES + h, zr, :, i * HD : (i + 1) * HD] = block


def call(kernel, outs, n_scalars, n_arrays, flops, size, scratch=()):
    return pl.pallas_call(
        kernel,
        out_shape=outs,
        in_specs=[SMEM] * n_scalars + [VMEM] * n_arrays,
        out_specs=[VMEM] * len(outs),
        scratch_shapes=list(scratch),
        compiler_params=pltpu.CompilerParams(vmem_limit_bytes=LIMIT),
        cost_estimate=pl.CostEstimate(flops=flops, bytes_accessed=size, transcendentals=0),
    )


def shaped(*shape):
    return jax.ShapeDtypeStruct(shape, jnp.bfloat16)


def local(text, feats, count, proj, gain, q_weight, k_weight, v_weight):
    zh, zl, y = lax.axis_index("zh"), lax.axis_index("zl"), lax.axis_index("y")
    core, section = lax.axis_index("core"), lax.axis_index("section")

    turned = jnp.bitwise_xor(jnp.arange(CHIP_ROWS, dtype=jnp.int32), core * ROWS)
    position = ((zh * ZL + zl) * Y + y) * CHIP_ROWS + turned
    ladder = jnp.arange(HD // 2, dtype=jnp.float32) * 2.0 / HD
    angle = position.astype(jnp.float32)[:, None] * (ROPE_BASE ** (-ladder))[None, :]
    cosine = jnp.cos(angle)
    sine = jnp.sin(angle)
    cosine = jnp.concatenate([cosine, cosine], axis=-1)
    sine = jnp.concatenate([-sine, sine], axis=-1)
    gains = gain.astype(jnp.float32).reshape(SECTIONS, TP, 512)
    gains = jnp.where(section == 0, gains, gains[::-1]).reshape(8, 512)
    feats_b = swap(feats, "section")
    weight = pl.pallas_call(
        join_kernel,
        out_shape=shaped(64, 6 * HD),
        in_specs=[pl.BlockSpec(memory_space=pl.ANY)] * 3,
        out_specs=VMEM,
        scratch_shapes=[pltpu.SemaphoreType.DMA((3,))],
        cost_estimate=pl.CostEstimate(flops=0, bytes_accessed=200000, transcendentals=0),
    )(q_weight, k_weight, v_weight)
    weight_b = swap(weight, "zh")

    weight_b, feats_b = lax.optimization_barrier((weight_b, feats_b))
    (weight,) = call(spread_kernel, [shaped(ZL * CORES, ZH, 64, 3 * HD)], 0, 2, 1000, 1 << 20)(
        weight, weight_b
    )
    weight = lax.all_to_all(weight, ("zl", "core"), 0, 0, tiled=True)

    feats = lax.all_gather(jnp.stack([feats, feats_b]), "tp", axis=0)
    (joined,) = call(join_frames_kernel, [shaped(ROWS, 512)], 1, 3, 2 * ROWS * 1024 * 512, 2 << 20)(
        jnp.stack([section, count[0]]), feats, proj.reshape(8, HD, 512), text
    )

    weight, joined = lax.optimization_barrier((weight, joined))
    weight = lax.all_gather(weight, "y", axis=0)
    joined_b = swap(joined, "section")
    own_a = lax.all_gather(joined, "tp", axis=0)
    own_a, joined_b = lax.optimization_barrier((own_a, joined_b))
    other_a = swap(own_a, "core")
    own_b = lax.all_gather(joined_b, "tp", axis=0)
    other_b = swap(own_b, "core")
    queries, kv, lines = pl.pallas_call(
        project_kernel,
        out_shape=[
            shaped(CHIP_ROWS, HD),
            shaped(CHIP_ROWS, 2 * HD),
            shaped(ZL, CHIP_ROWS, 2 * HD),
        ],
        in_specs=[SMEM] + [VMEM] * 4 + [pl.BlockSpec(memory_space=pltpu.HBM)] + [VMEM] * 3,
        out_specs=[VMEM] * 3,
        scratch_shapes=[
            pltpu.VMEM((Y, ZL * CORES, ZH, 64, 3 * HD), jnp.bfloat16),
            pltpu.SemaphoreType.DMA((TP,)),
        ],
        compiler_params=pltpu.CompilerParams(vmem_limit_bytes=LIMIT),
        cost_estimate=pl.CostEstimate(
            flops=2 * CHIP_ROWS * 4096 * 3 * HD, bytes_accessed=6 << 20, transcendentals=0
        ),
    )(
        jnp.bitwise_xor(zh, section).reshape(1),
        own_a,
        own_b,
        other_a,
        other_b,
        pltpu.with_memory_space_constraint(weight, pltpu.HBM),
        gains,
        cosine,
        sine,
    )

    kv_b = swap(kv, "zh")
    kv_a = lax.all_to_all(lines, "zl", 0, 0, tiled=True)
    queries = lax.all_gather(queries, "y", axis=0)
    kv_a, kv_b, queries = lax.optimization_barrier((kv_a, kv_b, queries))
    place = jnp.stack([zh, zl, y, core])
    scores = [pltpu.VMEM((Y, ZL, CHIP_ROWS, CHIP_ROWS), jnp.float32)]
    state = [jax.ShapeDtypeStruct((Y, CHIP_ROWS, HD), jnp.float32)] * 2
    flops = 4 * 1024 * 1024 * HD
    parts, levels = call(attend_own_kernel, state, 1, 2, flops, 2 << 20, scores)(
        place, queries, kv_a
    )
    kv_b = gather(kv_b, "zl", ZL)
    (parts,) = call(
        attend_rest_kernel, [shaped(Y * CORES, ROWS + 8, HD)], 1, 4, flops, 2 << 20, scores
    )(place, queries, kv_b, parts, levels)

    parts = lax.all_to_all(parts, ("y", "core"), 0, 0, tiled=True)
    (result,) = call(merge_kernel, [shaped(ROWS, 2 * HD)], 0, 1, 1 << 20, 1 << 20)(parts)
    return result


def solution(mesh):
    fine = Mesh(
        mesh.devices.reshape(ZH, ZL, Y, CORES, SECTIONS, TP),
        ("zh", "zl", "y", "core", "section", "tp"),
    )
    ctx = ("zh", "zl", "y", "core")
    in_specs = (P(ctx, F), P(ctx, F), P(ctx), P(None, F), P(), P(ctx, F), P(ctx, F), P(ctx, F))
    return jax.shard_map(
        local, mesh=fine, in_specs=in_specs, out_specs=P(ctx, F), check_vma=False
    )
```

```python
import math

import jax
import jax.numpy as jnp
from jax import lax
from jax.experimental import pallas as pl
from jax.experimental.pallas import tpu as pltpu
from jax.sharding import Mesh, PartitionSpec as P

HD = 128
ROPE_BASE = 1000000.0
NORM_EPS = 1e-05
MASKED = -1e30

ZH, ZL, Y, CORES, SECTIONS, TP = 2, 4, 4, 2, 2, 4
F = ("section", "tp")
ROWS = 128
CHIP_ROWS = 2 * ROWS
SWAP = [(0, 1), (1, 0)]
VMEM = pl.BlockSpec(memory_space=pltpu.VMEM)
SMEM = pl.BlockSpec(memory_space=pltpu.SMEM)
LIMIT = 40 << 20


def swap(v, axis):
    return lax.ppermute(v, axis, SWAP)


def gather(v, axis, n):
    return lax.all_to_all(jnp.broadcast_to(v[None], (n, *v.shape)), axis, 0, 0, tiled=True)


def join_frames_kernel(pick, feats, proj, text, out):
    vision = jnp.zeros((ROWS, 512), jnp.float32)
    for s in range(SECTIONS):
        first = jnp.bitwise_xor(pick[0], s) * TP
        for t in range(TP):
            vision = vision + jnp.dot(
                feats[t, s], proj[first + t], preferred_element_type=jnp.float32
            )
    row = lax.broadcasted_iota(jnp.int32, (ROWS, 512), 0)
    joined = jnp.where(row < pick[1], vision, text[...].astype(jnp.float32))
    out[...] = joined.astype(jnp.bfloat16)


def project_kernel(
    flip, own_a, own_b, other_a, other_b, stored, gain, cosine, sine, q_out, kv_out, lines_out, weight, sem
):
    copies = [
        pltpu.make_async_copy(
            stored.at[:, :, t * CORES : (t + 1) * CORES],
            weight.at[:, :, t * CORES : (t + 1) * CORES],
            sem.at[t],
        )
        for t in range(TP)
    ]
    for copy in copies:
        copy.start()
    tiles = [(own, other, t) for own, other in ((own_a, other_a), (own_b, other_b)) for t in range(TP)]
    squares = jnp.zeros((CHIP_ROWS, 512), jnp.float32)
    for own, other, t in tiles:
        wide = jnp.concatenate([own[t], other[t]], axis=0).astype(jnp.float32)
        squares = squares + wide * wide
    mean_square = jnp.sum(squares, axis=-1, keepdims=True) * (1.0 / 4096)
    inverse = lax.rsqrt(mean_square + NORM_EPS)
    total = jnp.zeros((CHIP_ROWS, 3 * HD), jnp.float32)
    for i, (own, other, t) in enumerate(tiles):
        if i < TP:
            copies[i].wait()
        half = jnp.bitwise_xor(flip[0], i // TP)
        wide = jnp.concatenate([own[t], other[t]], axis=0).astype(jnp.float32)
        normed = (wide * inverse * gain[i : i + 1, :]).astype(jnp.bfloat16)
        block = jnp.concatenate(
            [weight[y, half, t * CORES + c] for y in range(Y) for c in range(CORES)], axis=0
        )
        total = total + jnp.dot(normed, block, preferred_element_type=jnp.float32)
    q = total[:, :HD]
    k = total[:, HD : 2 * HD]
    cos, sin = cosine[...], sine[...]
    q_out[...] = (q * cos + pltpu.roll(q, HD // 2, 1) * sin).astype(jnp.bfloat16)
    k = (k * cos + pltpu.roll(k, HD // 2, 1) * sin).astype(jnp.bfloat16)
    v = total[:, 2 * HD :].astype(jnp.bfloat16)
    kv_out[:, :HD] = k
    kv_out[:, HD:] = v
    for i in range(ZL):
        lines_out[i, :, :HD] = k
        lines_out[i, :, HD:] = v


def encode(level):
    lane = lax.broadcasted_iota(jnp.int32, (CHIP_ROWS, HD), 1)
    high = level.astype(jnp.bfloat16).astype(jnp.float32)
    rest = level - high
    middle = rest.astype(jnp.bfloat16).astype(jnp.float32)
    low = rest - middle
    coded = jnp.where(
        lane == 0, high, jnp.where(lane == 1, middle, jnp.where(lane == 2, low, 0.0))
    ).astype(jnp.bfloat16)
    pick = lax.broadcasted_iota(jnp.int32, (8, HD), 0) == lax.broadcasted_iota(jnp.int32, (8, HD), 1)
    pick = pick.astype(jnp.float32).astype(jnp.bfloat16)
    coded = lax.dot_general(
        pick, coded, (((1,), (1,)), ((), ())), preferred_element_type=jnp.float32
    )
    return jnp.concatenate([coded[:, :ROWS], coded[:, ROWS:]], axis=0).astype(jnp.bfloat16)


def attend(q, kv, scores, mask):
    shape = (CHIP_ROWS, CHIP_ROWS)
    scale = 1.0 / math.sqrt(HD)
    peak = jnp.full(shape, MASKED, jnp.float32)
    for l in range(ZL):
        s = lax.dot_general(
            q, kv[l, :, :HD], (((1,), (1,)), ((), ())), preferred_element_type=jnp.float32
        )
        s = mask(l, s * scale)
        scores[l] = s
        peak = jnp.maximum(peak, s)
    best = jnp.max(peak, axis=-1, keepdims=True)
    mass = jnp.zeros(shape, jnp.float32)
    part = jnp.zeros((CHIP_ROWS, HD), jnp.float32)
    for l in range(ZL):
        w = jnp.exp(scores[l] - best)
        mass = mass + w
        part = part + jnp.dot(
            w.astype(jnp.bfloat16), kv[l, :, HD:], preferred_element_type=jnp.float32
        )
    total = jnp.sum(mass, axis=-1, keepdims=True)
    return part / total, jnp.where(best > 0.5 * MASKED, best + jnp.log(total), MASKED)


def attend_own_kernel(place, queries, kv, parts, levels, scores):
    zl, me, core = place[1], place[2], place[3]
    shape = (CHIP_ROWS, CHIP_ROWS)
    turn = core * ROWS
    row = jnp.bitwise_xor(lax.broadcasted_iota(jnp.int32, shape, 0), turn)
    col = jnp.bitwise_xor(lax.broadcasted_iota(jnp.int32, shape, 1), turn)
    ahead = col - row

    def one(pair, carry):
        for i in range(2):
            y = pair * 2 + i

            def mask(l, s):
                return jnp.where(ahead <= ((zl - l) * Y + y - me) * CHIP_ROWS, s, MASKED)

            part, level = attend(queries[y], kv, scores.at[i], mask)
            parts[y] = part
            levels[y] = jnp.broadcast_to(level, (CHIP_ROWS, HD))
        return carry

    lax.fori_loop(0, Y // 2, one, 0)


def attend_rest_kernel(place, queries, kv, parts, levels, out, scores):
    def put(y, part, level):
        coded = encode(level)
        part = part.astype(jnp.bfloat16)
        for i in range(CORES):
            owner = y * CORES + jnp.bitwise_xor(place[3], i)
            out[owner, :ROWS, :] = part[i * ROWS : (i + 1) * ROWS]
            out[owner, ROWS:, :] = coded[i * 8 : (i + 1) * 8]

    @pl.when(place[0] == 0)
    def _():
        for y in range(Y):
            put(y, parts[y], levels[y, :, 0:1])

    @pl.when(place[0] != 0)
    def _():
        for y in range(Y):
            part, level = attend(queries[y], kv, scores.at[y], lambda l, s: s)
            before = levels[y, :, 0:1]
            top = jnp.maximum(level, before)
            new, old = jnp.exp(level - top), jnp.exp(before - top)
            total = new + old
            put(y, (part * new + parts[y] * old) / total, top + jnp.log(total))


def merge_kernel(parts, out):
    shares = []
    for h in range(CORES):
        levels = []
        for y in range(Y):
            coded = parts[y * CORES + h, ROWS:, :].astype(jnp.float32)
            levels.append(coded[0:1] + coded[1:2] + coded[2:3])
        levels = jnp.concatenate(levels, axis=0)
        share = jnp.exp(levels - jnp.max(levels, axis=0, keepdims=True))
        shares.append(share / jnp.sum(share, axis=0, keepdims=True))
    shares = jnp.transpose(jnp.concatenate(shares * (ROWS // (CORES * Y)), axis=0))
    for h in range(CORES):
        result = jnp.zeros((ROWS, HD), jnp.float32)
        for y in range(Y):
            lane = h * Y + y
            block = parts[y * CORES + h, :ROWS, :].astype(jnp.float32)
            result = result + shares[:, lane : lane + 1] * block
        out[:, h * HD : (h + 1) * HD] = result.astype(jnp.bfloat16)


def spread_kernel(w, out):
    for h in range(CORES):
        for i in range(3):
            block = w[:, (2 * i + h) * HD : (2 * i + h + 1) * HD]
            for l in range(ZL):
                out[l * CORES + h, :, i * HD : (i + 1) * HD] = block


def join_kernel(q, k, v, joined, out, sems):
    copies = [
        pltpu.make_async_copy(w, joined.at[:, i * 2 * HD : (i + 1) * 2 * HD], sems.at[i])
        for i, w in enumerate((q, k, v))
    ]
    for copy in copies:
        copy.start()
    for copy in copies:
        copy.wait()
    spread_kernel(joined, out)


def call(kernel, outs, n_scalars, n_arrays, flops, size, scratch=()):
    return pl.pallas_call(
        kernel,
        out_shape=outs,
        in_specs=[SMEM] * n_scalars + [VMEM] * n_arrays,
        out_specs=[VMEM] * len(outs),
        scratch_shapes=list(scratch),
        compiler_params=pltpu.CompilerParams(vmem_limit_bytes=LIMIT),
        cost_estimate=pl.CostEstimate(flops=flops, bytes_accessed=size, transcendentals=0),
    )


def shaped(*shape):
    return jax.ShapeDtypeStruct(shape, jnp.bfloat16)


def local(text, feats, count, proj, gain, q_weight, k_weight, v_weight):
    zh, zl, y = lax.axis_index("zh"), lax.axis_index("zl"), lax.axis_index("y")
    core, section = lax.axis_index("core"), lax.axis_index("section")

    turned = jnp.bitwise_xor(jnp.arange(CHIP_ROWS, dtype=jnp.int32), core * ROWS)
    position = ((zh * ZL + zl) * Y + y) * CHIP_ROWS + turned
    ladder = jnp.arange(HD // 2, dtype=jnp.float32) * 2.0 / HD
    angle = position.astype(jnp.float32)[:, None] * (ROPE_BASE ** (-ladder))[None, :]
    cosine = jnp.cos(angle)
    sine = jnp.sin(angle)
    cosine = jnp.concatenate([cosine, cosine], axis=-1)
    sine = jnp.concatenate([-sine, sine], axis=-1)
    gains = gain.astype(jnp.float32).reshape(SECTIONS, TP, 512)
    gains = jnp.where(section == 0, gains, gains[::-1]).reshape(8, 512)
    feats_b = swap(feats, "section")
    weight, spread = pl.pallas_call(
        join_kernel,
        out_shape=[shaped(64, 6 * HD), shaped(ZL * CORES, 64, 3 * HD)],
        in_specs=[pl.BlockSpec(memory_space=pl.ANY)] * 3,
        out_specs=[VMEM] * 2,
        scratch_shapes=[pltpu.SemaphoreType.DMA((3,))],
        cost_estimate=pl.CostEstimate(flops=0, bytes_accessed=800000, transcendentals=0),
    )(q_weight, k_weight, v_weight)
    weight_b = swap(weight, "zh")
    weight_a = lax.all_to_all(spread, ("zl", "core"), 0, 0, tiled=True)
    weight_a, weight_b, feats_b = lax.optimization_barrier((weight_a, weight_b, feats_b))
    (spread,) = call(spread_kernel, [shaped(ZL * CORES, 64, 3 * HD)], 0, 1, 1000, 1 << 20)(weight_b)
    weight_b = lax.all_to_all(spread, ("zl", "core"), 0, 0, tiled=True)

    feats = lax.all_gather(jnp.stack([feats, feats_b]), "tp", axis=0)
    weight_b, feats = lax.optimization_barrier((weight_b, feats))
    weight = lax.all_gather(jnp.stack([weight_a, weight_b]), "y", axis=0)
    (joined,) = call(join_frames_kernel, [shaped(ROWS, 512)], 1, 3, 2 * ROWS * 1024 * 512, 2 << 20)(
        jnp.stack([section, count[0]]), feats, proj.reshape(8, HD, 512), text
    )

    joined_b = swap(joined, "section")
    own_a = lax.all_gather(joined, "tp", axis=0)
    own_a, joined_b = lax.optimization_barrier((own_a, joined_b))
    other_a = swap(own_a, "core")
    own_b = lax.all_gather(joined_b, "tp", axis=0)
    other_b = swap(own_b, "core")
    queries, kv, lines = pl.pallas_call(
        project_kernel,
        out_shape=[
            shaped(CHIP_ROWS, HD),
            shaped(CHIP_ROWS, 2 * HD),
            shaped(ZL, CHIP_ROWS, 2 * HD),
        ],
        in_specs=[SMEM] + [VMEM] * 4 + [pl.BlockSpec(memory_space=pltpu.HBM)] + [VMEM] * 3,
        out_specs=[VMEM] * 3,
        scratch_shapes=[
            pltpu.VMEM((Y, ZH, ZL * CORES, 64, 3 * HD), jnp.bfloat16),
            pltpu.SemaphoreType.DMA((TP,)),
        ],
        compiler_params=pltpu.CompilerParams(vmem_limit_bytes=LIMIT),
        cost_estimate=pl.CostEstimate(
            flops=2 * CHIP_ROWS * 4096 * 3 * HD, bytes_accessed=6 << 20, transcendentals=0
        ),
    )(
        jnp.bitwise_xor(zh, section).reshape(1),
        own_a,
        own_b,
        other_a,
        other_b,
        pltpu.with_memory_space_constraint(weight, pltpu.HBM),
        gains,
        cosine,
        sine,
    )

    kv_b = swap(kv, "zh")
    kv_a = lax.all_to_all(lines, "zl", 0, 0, tiled=True)
    queries = lax.all_gather(queries, "y", axis=0)
    kv_a, kv_b, queries = lax.optimization_barrier((kv_a, kv_b, queries))
    place = jnp.stack([zh, zl, y, core])
    scores = [pltpu.VMEM((Y, ZL, CHIP_ROWS, CHIP_ROWS), jnp.float32)]
    state = [jax.ShapeDtypeStruct((Y, CHIP_ROWS, HD), jnp.float32)] * 2
    flops = 4 * 1024 * 1024 * HD
    parts, levels = call(attend_own_kernel, state, 1, 2, flops, 2 << 20, scores)(
        place, queries, kv_a
    )
    kv_b = gather(kv_b, "zl", ZL)
    (parts,) = call(
        attend_rest_kernel, [shaped(Y * CORES, ROWS + 8, HD)], 1, 4, flops, 2 << 20, scores
    )(place, queries, kv_b, parts, levels)

    parts = lax.all_to_all(parts, ("y", "core"), 0, 0, tiled=True)
    (result,) = call(merge_kernel, [shaped(ROWS, 2 * HD)], 0, 1, 1 << 20, 1 << 20)(parts)
    return result


def solution(mesh):
    fine = Mesh(
        mesh.devices.reshape(ZH, ZL, Y, CORES, SECTIONS, TP),
        ("zh", "zl", "y", "core", "section", "tp"),
    )
    ctx = ("zh", "zl", "y", "core")
    in_specs = (P(ctx, F), P(ctx, F), P(ctx), P(None, F), P(), P(ctx, F), P(ctx, F), P(ctx, F))
    return jax.shard_map(
        local, mesh=fine, in_specs=in_specs, out_specs=P(ctx, F), check_vma=False
    )
```

```python
import math

import jax
import jax.numpy as jnp
from jax import lax
from jax.experimental import pallas as pl
from jax.experimental.pallas import tpu as pltpu
from jax.sharding import Mesh, PartitionSpec as P

HD = 128
ROPE_BASE = 1000000.0
NORM_EPS = 1e-05
MASKED = -1e30

ZH, ZL, Y, CORES, SECTIONS, TP = 2, 4, 4, 2, 2, 4
F = ("section", "tp")
ROWS = 128
CHIP_ROWS = 2 * ROWS
SWAP = [(0, 1), (1, 0)]
VMEM = pl.BlockSpec(memory_space=pltpu.VMEM)
SMEM = pl.BlockSpec(memory_space=pltpu.SMEM)
LIMIT = 40 << 20


def swap(v, axis):
    return lax.ppermute(v, axis, SWAP)


def gather(v, axis, n):
    return lax.all_to_all(jnp.broadcast_to(v[None], (n, *v.shape)), axis, 0, 0, tiled=True)


def join_frames_kernel(pick, feats_a, feats_b, proj, text, out):
    vision = jnp.zeros((ROWS, 512), jnp.float32)
    for s, feats in enumerate((feats_a, feats_b)):
        first = jnp.bitwise_xor(pick[0], s) * TP
        for t in range(TP):
            vision = vision + jnp.dot(
                feats[t], proj[first + t], preferred_element_type=jnp.float32
            )
    row = lax.broadcasted_iota(jnp.int32, (ROWS, 512), 0)
    joined = jnp.where(row < pick[1], vision, text[...].astype(jnp.float32))
    out[...] = joined.astype(jnp.bfloat16)


def project_kernel(
    flip, own_a, own_b, other_a, other_b, stored, gain, cosine, sine, q_out, kv_out, lines_out, weight, sem
):
    copies = [
        pltpu.make_async_copy(
            stored.at[:, :, t * CORES : (t + 1) * CORES],
            weight.at[:, :, t * CORES : (t + 1) * CORES],
            sem.at[t],
        )
        for t in range(TP)
    ]
    for copy in copies:
        copy.start()
    tiles = [(own, other, t) for own, other in ((own_a, other_a), (own_b, other_b)) for t in range(TP)]
    squares = jnp.zeros((CHIP_ROWS, 512), jnp.float32)
    for own, other, t in tiles:
        wide = jnp.concatenate([own[t], other[t]], axis=0).astype(jnp.float32)
        squares = squares + wide * wide
    mean_square = jnp.sum(squares, axis=-1, keepdims=True) * (1.0 / 4096)
    inverse = lax.rsqrt(mean_square + NORM_EPS)
    total = jnp.zeros((CHIP_ROWS, 3 * HD), jnp.float32)
    for i, (own, other, t) in enumerate(tiles):
        if i < TP:
            copies[i].wait()
        half = jnp.bitwise_xor(flip[0], i // TP)
        wide = jnp.concatenate([own[t], other[t]], axis=0).astype(jnp.float32)
        normed = (wide * inverse * gain[i : i + 1, :]).astype(jnp.bfloat16)
        block = jnp.concatenate(
            [weight[y, half, t * CORES + c] for y in range(Y) for c in range(CORES)], axis=0
        )
        total = total + jnp.dot(normed, block, preferred_element_type=jnp.float32)
    q = total[:, :HD]
    k = total[:, HD : 2 * HD]
    cos, sin = cosine[...], sine[...]
    q_out[...] = (q * cos + pltpu.roll(q, HD // 2, 1) * sin).astype(jnp.bfloat16)
    k = (k * cos + pltpu.roll(k, HD // 2, 1) * sin).astype(jnp.bfloat16)
    v = total[:, 2 * HD :].astype(jnp.bfloat16)
    kv_out[:, :HD] = k
    kv_out[:, HD:] = v
    for i in range(ZL):
        lines_out[i, :, :HD] = k
        lines_out[i, :, HD:] = v


def encode(level):
    lane = lax.broadcasted_iota(jnp.int32, (CHIP_ROWS, HD), 1)
    high = level.astype(jnp.bfloat16).astype(jnp.float32)
    rest = level - high
    middle = rest.astype(jnp.bfloat16).astype(jnp.float32)
    low = rest - middle
    coded = jnp.where(
        lane == 0, high, jnp.where(lane == 1, middle, jnp.where(lane == 2, low, 0.0))
    ).astype(jnp.bfloat16)
    pick = lax.broadcasted_iota(jnp.int32, (8, HD), 0) == lax.broadcasted_iota(jnp.int32, (8, HD), 1)
    pick = pick.astype(jnp.float32).astype(jnp.bfloat16)
    coded = lax.dot_general(
        pick, coded, (((1,), (1,)), ((), ())), preferred_element_type=jnp.float32
    )
    return jnp.concatenate([coded[:, :ROWS], coded[:, ROWS:]], axis=0).astype(jnp.bfloat16)


def attend(q, kv, scores, mask):
    shape = (CHIP_ROWS, CHIP_ROWS)
    scale = 1.0 / math.sqrt(HD)
    peak = jnp.full(shape, MASKED, jnp.float32)
    for l in range(ZL):
        s = lax.dot_general(
            q, kv[l, :, :HD], (((1,), (1,)), ((), ())), preferred_element_type=jnp.float32
        )
        s = mask(l, s * scale)
        scores[l] = s
        peak = jnp.maximum(peak, s)
    best = jnp.max(peak, axis=-1, keepdims=True)
    mass = jnp.zeros(shape, jnp.float32)
    part = jnp.zeros((CHIP_ROWS, HD), jnp.float32)
    for l in range(ZL):
        w = jnp.exp(scores[l] - best)
        mass = mass + w
        part = part + jnp.dot(
            w.astype(jnp.bfloat16), kv[l, :, HD:], preferred_element_type=jnp.float32
        )
    total = jnp.sum(mass, axis=-1, keepdims=True)
    return part / total, jnp.where(best > 0.5 * MASKED, best + jnp.log(total), MASKED)


def attend_own_kernel(place, queries, kv, parts, levels, scores):
    zl, me, core = place[1], place[2], place[3]
    shape = (CHIP_ROWS, CHIP_ROWS)
    turn = core * ROWS
    row = jnp.bitwise_xor(lax.broadcasted_iota(jnp.int32, shape, 0), turn)
    col = jnp.bitwise_xor(lax.broadcasted_iota(jnp.int32, shape, 1), turn)
    ahead = col - row

    def one(pair, carry):
        for i in range(2):
            y = pair * 2 + i

            def mask(l, s):
                return jnp.where(ahead <= ((zl - l) * Y + y - me) * CHIP_ROWS, s, MASKED)

            part, level = attend(queries[y], kv, scores.at[i], mask)
            parts[y] = part
            levels[y] = jnp.broadcast_to(level, (CHIP_ROWS, HD))
        return carry

    lax.fori_loop(0, Y // 2, one, 0)


def attend_rest_kernel(place, queries, kv, parts, levels, out, scores):
    def put(y, part, level):
        coded = encode(level)
        part = part.astype(jnp.bfloat16)
        for i in range(CORES):
            owner = y * CORES + jnp.bitwise_xor(place[3], i)
            out[owner, :ROWS, :] = part[i * ROWS : (i + 1) * ROWS]
            out[owner, ROWS:, :] = coded[i * 8 : (i + 1) * 8]

    @pl.when(place[0] == 0)
    def _():
        for y in range(Y):
            put(y, parts[y], levels[y, :, 0:1])

    @pl.when(place[0] != 0)
    def _():
        for y in range(Y):
            part, level = attend(queries[y], kv, scores.at[y], lambda l, s: s)
            before = levels[y, :, 0:1]
            top = jnp.maximum(level, before)
            new, old = jnp.exp(level - top), jnp.exp(before - top)
            total = new + old
            put(y, (part * new + parts[y] * old) / total, top + jnp.log(total))


def merge_kernel(parts, out):
    shares = []
    for h in range(CORES):
        levels = []
        for y in range(Y):
            coded = parts[y * CORES + h, ROWS:, :].astype(jnp.float32)
            levels.append(coded[0:1] + coded[1:2] + coded[2:3])
        levels = jnp.concatenate(levels, axis=0)
        share = jnp.exp(levels - jnp.max(levels, axis=0, keepdims=True))
        shares.append(share / jnp.sum(share, axis=0, keepdims=True))
    shares = jnp.transpose(jnp.concatenate(shares * (ROWS // (CORES * Y)), axis=0))
    for h in range(CORES):
        result = jnp.zeros((ROWS, HD), jnp.float32)
        for y in range(Y):
            lane = h * Y + y
            block = parts[y * CORES + h, :ROWS, :].astype(jnp.float32)
            result = result + shares[:, lane : lane + 1] * block
        out[:, h * HD : (h + 1) * HD] = result.astype(jnp.bfloat16)


def spread_kernel(w, out):
    for h in range(CORES):
        for i in range(3):
            block = w[:, (2 * i + h) * HD : (2 * i + h + 1) * HD]
            for l in range(ZL):
                out[l * CORES + h, :, i * HD : (i + 1) * HD] = block


def join_kernel(q, k, v, joined, out, sems):
    copies = [
        pltpu.make_async_copy(w, joined.at[:, i * 2 * HD : (i + 1) * 2 * HD], sems.at[i])
        for i, w in enumerate((q, k, v))
    ]
    for copy in copies:
        copy.start()
    for copy in copies:
        copy.wait()
    spread_kernel(joined, out)


def call(kernel, outs, n_scalars, n_arrays, flops, size, scratch=()):
    return pl.pallas_call(
        kernel,
        out_shape=outs,
        in_specs=[SMEM] * n_scalars + [VMEM] * n_arrays,
        out_specs=[VMEM] * len(outs),
        scratch_shapes=list(scratch),
        compiler_params=pltpu.CompilerParams(vmem_limit_bytes=LIMIT),
        cost_estimate=pl.CostEstimate(flops=flops, bytes_accessed=size, transcendentals=0),
    )


def shaped(*shape):
    return jax.ShapeDtypeStruct(shape, jnp.bfloat16)


def local(text, feats, count, proj, gain, q_weight, k_weight, v_weight):
    zh, zl, y = lax.axis_index("zh"), lax.axis_index("zl"), lax.axis_index("y")
    core, section = lax.axis_index("core"), lax.axis_index("section")

    turned = jnp.bitwise_xor(jnp.arange(CHIP_ROWS, dtype=jnp.int32), core * ROWS)
    position = ((zh * ZL + zl) * Y + y) * CHIP_ROWS + turned
    ladder = jnp.arange(HD // 2, dtype=jnp.float32) * 2.0 / HD
    angle = position.astype(jnp.float32)[:, None] * (ROPE_BASE ** (-ladder))[None, :]
    cosine = jnp.cos(angle)
    sine = jnp.sin(angle)
    cosine = jnp.concatenate([cosine, cosine], axis=-1)
    sine = jnp.concatenate([-sine, sine], axis=-1)
    gains = gain.astype(jnp.float32).reshape(SECTIONS, TP, 512)
    gains = jnp.where(section == 0, gains, gains[::-1]).reshape(8, 512)
    feats_b = swap(feats, "section")
    weight, spread = pl.pallas_call(
        join_kernel,
        out_shape=[shaped(64, 6 * HD), shaped(ZL * CORES, 64, 3 * HD)],
        in_specs=[pl.BlockSpec(memory_space=pl.ANY)] * 3,
        out_specs=[VMEM] * 2,
        scratch_shapes=[pltpu.SemaphoreType.DMA((3,))],
        cost_estimate=pl.CostEstimate(flops=0, bytes_accessed=800000, transcendentals=0),
    )(q_weight, k_weight, v_weight)
    weight_b = swap(weight, "zh")
    weight_a = lax.all_to_all(spread, ("zl", "core"), 0, 0, tiled=True)
    feats_a = lax.all_gather(feats, "tp", axis=0)
    weight_a, weight_b, feats_a, feats_b = lax.optimization_barrier(
        (weight_a, weight_b, feats_a, feats_b)
    )
    (spread,) = call(spread_kernel, [shaped(ZL * CORES, 64, 3 * HD)], 0, 1, 1000, 1 << 20)(weight_b)
    weight_b = lax.all_to_all(spread, ("zl", "core"), 0, 0, tiled=True)

    feats_b = lax.all_gather(feats_b, "tp", axis=0)
    weight_b, feats_b = lax.optimization_barrier((weight_b, feats_b))
    weight = lax.all_gather(jnp.stack([weight_a, weight_b]), "y", axis=0)
    (joined,) = call(join_frames_kernel, [shaped(ROWS, 512)], 1, 4, 2 * ROWS * 1024 * 512, 2 << 20)(
        jnp.stack([section, count[0]]), feats_a, feats_b, proj.reshape(8, HD, 512), text
    )

    joined_b = swap(joined, "section")
    own_a = lax.all_gather(joined, "tp", axis=0)
    own_a, joined_b = lax.optimization_barrier((own_a, joined_b))
    other_a = swap(own_a, "core")
    own_b = lax.all_gather(joined_b, "tp", axis=0)
    other_b = swap(own_b, "core")
    queries, kv, lines = pl.pallas_call(
        project_kernel,
        out_shape=[
            shaped(CHIP_ROWS, HD),
            shaped(CHIP_ROWS, 2 * HD),
            shaped(ZL, CHIP_ROWS, 2 * HD),
        ],
        in_specs=[SMEM] + [VMEM] * 4 + [pl.BlockSpec(memory_space=pltpu.HBM)] + [VMEM] * 3,
        out_specs=[VMEM] * 3,
        scratch_shapes=[
            pltpu.VMEM((Y, ZH, ZL * CORES, 64, 3 * HD), jnp.bfloat16),
            pltpu.SemaphoreType.DMA((TP,)),
        ],
        compiler_params=pltpu.CompilerParams(vmem_limit_bytes=LIMIT),
        cost_estimate=pl.CostEstimate(
            flops=2 * CHIP_ROWS * 4096 * 3 * HD, bytes_accessed=6 << 20, transcendentals=0
        ),
    )(
        jnp.bitwise_xor(zh, section).reshape(1),
        own_a,
        own_b,
        other_a,
        other_b,
        pltpu.with_memory_space_constraint(weight, pltpu.HBM),
        gains,
        cosine,
        sine,
    )

    kv_b = swap(kv, "zh")
    kv_a = lax.all_to_all(lines, "zl", 0, 0, tiled=True)
    queries = lax.all_gather(queries, "y", axis=0)
    kv_a, kv_b, queries = lax.optimization_barrier((kv_a, kv_b, queries))
    place = jnp.stack([zh, zl, y, core])
    scores = [pltpu.VMEM((Y, ZL, CHIP_ROWS, CHIP_ROWS), jnp.float32)]
    state = [jax.ShapeDtypeStruct((Y, CHIP_ROWS, HD), jnp.float32)] * 2
    flops = 4 * 1024 * 1024 * HD
    parts, levels = call(attend_own_kernel, state, 1, 2, flops, 2 << 20, scores)(
        place, queries, kv_a
    )
    kv_b = gather(kv_b, "zl", ZL)
    (parts,) = call(
        attend_rest_kernel, [shaped(Y * CORES, ROWS + 8, HD)], 1, 4, flops, 2 << 20, scores
    )(place, queries, kv_b, parts, levels)

    parts = lax.all_to_all(parts, ("y", "core"), 0, 0, tiled=True)
    (result,) = call(merge_kernel, [shaped(ROWS, 2 * HD)], 0, 1, 1 << 20, 1 << 20)(parts)
    return result


def solution(mesh):
    fine = Mesh(
        mesh.devices.reshape(ZH, ZL, Y, CORES, SECTIONS, TP),
        ("zh", "zl", "y", "core", "section", "tp"),
    )
    ctx = ("zh", "zl", "y", "core")
    in_specs = (P(ctx, F), P(ctx, F), P(ctx), P(None, F), P(), P(ctx, F), P(ctx, F), P(ctx, F))
    return jax.shard_map(
        local, mesh=fine, in_specs=in_specs, out_specs=P(ctx, F), check_vma=False
    )
```

```python
import math

import jax
import jax.numpy as jnp
from jax import lax
from jax.experimental import pallas as pl
from jax.experimental.pallas import tpu as pltpu
from jax.sharding import Mesh, PartitionSpec as P

HD = 128
ROPE_BASE = 1000000.0
NORM_EPS = 1e-05
MASKED = -1e30

ZH, ZL, Y, CORES, SECTIONS, TP = 2, 4, 4, 2, 2, 4
F = ("section", "tp")
ROWS = 128
CHIP_ROWS = 2 * ROWS
SWAP = [(0, 1), (1, 0)]
VMEM = pl.BlockSpec(memory_space=pltpu.VMEM)
SMEM = pl.BlockSpec(memory_space=pltpu.SMEM)
LIMIT = 40 << 20


def swap(v, axis):
    return lax.ppermute(v, axis, SWAP)


def gather(v, axis, n):
    return lax.all_to_all(jnp.broadcast_to(v[None], (n, *v.shape)), axis, 0, 0, tiled=True)


def join_frames_kernel(pick, feats, proj, text, out):
    vision = jnp.zeros((ROWS, 512), jnp.float32)
    for s in range(SECTIONS):
        first = jnp.bitwise_xor(pick[0], s) * TP
        for t in range(TP):
            vision = vision + jnp.dot(
                feats[t, s], proj[first + t], preferred_element_type=jnp.float32
            )
    row = lax.broadcasted_iota(jnp.int32, (ROWS, 512), 0)
    joined = jnp.where(row < pick[1], vision, text[...].astype(jnp.float32))
    out[...] = joined.astype(jnp.bfloat16)


def project_kernel(
    flip, own_a, own_b, other_a, other_b, stored, gain, cosine, sine, q_out, kv_out, lines_out, weight, sem, normed
):
    copies = [
        pltpu.make_async_copy(
            stored.at[:, :, t * CORES : (t + 1) * CORES],
            weight.at[:, :, t * CORES : (t + 1) * CORES],
            sem.at[t],
        )
        for t in range(TP)
    ]
    for copy in copies:
        copy.start()
    tiles = [(own, other, t) for own, other in ((own_a, other_a), (own_b, other_b)) for t in range(TP)]
    squares = jnp.zeros((CHIP_ROWS, 512), jnp.float32)
    for own, other, t in tiles:
        wide = jnp.concatenate([own[t], other[t]], axis=0).astype(jnp.float32)
        squares = squares + wide * wide
    mean_square = jnp.sum(squares, axis=-1, keepdims=True) * (1.0 / 4096)
    inverse = lax.rsqrt(mean_square + NORM_EPS)
    for i, (own, other, t) in enumerate(tiles):
        wide = jnp.concatenate([own[t], other[t]], axis=0).astype(jnp.float32)
        normed[i] = (wide * inverse * gain[i : i + 1, :]).astype(jnp.bfloat16)
    for copy in copies:
        copy.wait()
    total = jnp.zeros((CHIP_ROWS, 3 * HD), jnp.float32)
    for i, (_, _, t) in enumerate(tiles):
        half = jnp.bitwise_xor(flip[0], i // TP)
        block = jnp.concatenate(
            [weight[y, half, t * CORES + c] for y in range(Y) for c in range(CORES)], axis=0
        )
        total = total + jnp.dot(normed[i], block, preferred_element_type=jnp.float32)
    q = total[:, :HD]
    k = total[:, HD : 2 * HD]
    cos, sin = cosine[...], sine[...]
    q_out[...] = (q * cos + pltpu.roll(q, HD // 2, 1) * sin).astype(jnp.bfloat16)
    k = (k * cos + pltpu.roll(k, HD // 2, 1) * sin).astype(jnp.bfloat16)
    v = total[:, 2 * HD :].astype(jnp.bfloat16)
    kv_out[:, :HD] = k
    kv_out[:, HD:] = v
    for i in range(ZL):
        lines_out[i, :, :HD] = k
        lines_out[i, :, HD:] = v


def encode(level):
    lane = lax.broadcasted_iota(jnp.int32, (CHIP_ROWS, HD), 1)
    high = level.astype(jnp.bfloat16).astype(jnp.float32)
    rest = level - high
    middle = rest.astype(jnp.bfloat16).astype(jnp.float32)
    low = rest - middle
    coded = jnp.where(
        lane == 0, high, jnp.where(lane == 1, middle, jnp.where(lane == 2, low, 0.0))
    ).astype(jnp.bfloat16)
    pick = lax.broadcasted_iota(jnp.int32, (8, HD), 0) == lax.broadcasted_iota(jnp.int32, (8, HD), 1)
    pick = pick.astype(jnp.float32).astype(jnp.bfloat16)
    coded = lax.dot_general(
        pick, coded, (((1,), (1,)), ((), ())), preferred_element_type=jnp.float32
    )
    return jnp.concatenate([coded[:, :ROWS], coded[:, ROWS:]], axis=0).astype(jnp.bfloat16)


def attend(q, kv, scores, mask):
    shape = (CHIP_ROWS, CHIP_ROWS)
    scale = 1.0 / math.sqrt(HD)
    peak = jnp.full(shape, MASKED, jnp.float32)
    for l in range(ZL):
        s = lax.dot_general(
            q, kv[l, :, :HD], (((1,), (1,)), ((), ())), preferred_element_type=jnp.float32
        )
        s = mask(l, s * scale)
        scores[l] = s
        peak = jnp.maximum(peak, s)
    best = jnp.max(peak, axis=-1, keepdims=True)
    mass = jnp.zeros(shape, jnp.float32)
    part = jnp.zeros((CHIP_ROWS, HD), jnp.float32)
    for l in range(ZL):
        w = jnp.exp(scores[l] - best)
        mass = mass + w
        part = part + jnp.dot(
            w.astype(jnp.bfloat16), kv[l, :, HD:], preferred_element_type=jnp.float32
        )
    total = jnp.sum(mass, axis=-1, keepdims=True)
    return part / total, jnp.where(best > 0.5 * MASKED, best + jnp.log(total), MASKED)


def attend_own_kernel(place, queries, kv, parts, levels, scores):
    zl, me, core = place[1], place[2], place[3]
    shape = (CHIP_ROWS, CHIP_ROWS)
    turn = core * ROWS
    row = jnp.bitwise_xor(lax.broadcasted_iota(jnp.int32, shape, 0), turn)
    col = jnp.bitwise_xor(lax.broadcasted_iota(jnp.int32, shape, 1), turn)
    ahead = col - row

    def one(pair, carry):
        for i in range(2):
            y = pair * 2 + i

            def mask(l, s):
                return jnp.where(ahead <= ((zl - l) * Y + y - me) * CHIP_ROWS, s, MASKED)

            part, level = attend(queries[y], kv, scores.at[i], mask)
            parts[y] = part
            levels[y] = jnp.broadcast_to(level, (CHIP_ROWS, HD))
        return carry

    lax.fori_loop(0, Y // 2, one, 0)


def attend_rest_kernel(place, queries, kv, parts, levels, out, scores):
    def put(y, part, level):
        coded = encode(level)
        part = part.astype(jnp.bfloat16)
        for i in range(CORES):
            owner = y * CORES + jnp.bitwise_xor(place[3], i)
            out[owner, :ROWS, :] = part[i * ROWS : (i + 1) * ROWS]
            out[owner, ROWS:, :] = coded[i * 8 : (i + 1) * 8]

    @pl.when(place[0] == 0)
    def _():
        for y in range(Y):
            put(y, parts[y], levels[y, :, 0:1])

    @pl.when(place[0] != 0)
    def _():
        for y in range(Y):
            part, level = attend(queries[y], kv, scores.at[y], lambda l, s: s)
            before = levels[y, :, 0:1]
            top = jnp.maximum(level, before)
            new, old = jnp.exp(level - top), jnp.exp(before - top)
            total = new + old
            put(y, (part * new + parts[y] * old) / total, top + jnp.log(total))


def merge_kernel(parts, out):
    shares = []
    for h in range(CORES):
        levels = []
        for y in range(Y):
            coded = parts[y * CORES + h, ROWS:, :].astype(jnp.float32)
            levels.append(coded[0:1] + coded[1:2] + coded[2:3])
        levels = jnp.concatenate(levels, axis=0)
        share = jnp.exp(levels - jnp.max(levels, axis=0, keepdims=True))
        shares.append(share / jnp.sum(share, axis=0, keepdims=True))
    shares = jnp.transpose(jnp.concatenate(shares * (ROWS // (CORES * Y)), axis=0))
    for h in range(CORES):
        result = jnp.zeros((ROWS, HD), jnp.float32)
        for y in range(Y):
            lane = h * Y + y
            block = parts[y * CORES + h, :ROWS, :].astype(jnp.float32)
            result = result + shares[:, lane : lane + 1] * block
        out[:, h * HD : (h + 1) * HD] = result.astype(jnp.bfloat16)


def spread_kernel(w, out):
    for h in range(CORES):
        for i in range(3):
            block = w[:, (2 * i + h) * HD : (2 * i + h + 1) * HD]
            for l in range(ZL):
                out[l * CORES + h, :, i * HD : (i + 1) * HD] = block


def join_kernel(q, k, v, joined, out, sems):
    copies = [
        pltpu.make_async_copy(w, joined.at[:, i * 2 * HD : (i + 1) * 2 * HD], sems.at[i])
        for i, w in enumerate((q, k, v))
    ]
    for copy in copies:
        copy.start()
    for copy in copies:
        copy.wait()
    spread_kernel(joined, out)


def call(kernel, outs, n_scalars, n_arrays, flops, size, scratch=()):
    return pl.pallas_call(
        kernel,
        out_shape=outs,
        in_specs=[SMEM] * n_scalars + [VMEM] * n_arrays,
        out_specs=[VMEM] * len(outs),
        scratch_shapes=list(scratch),
        compiler_params=pltpu.CompilerParams(vmem_limit_bytes=LIMIT),
        cost_estimate=pl.CostEstimate(flops=flops, bytes_accessed=size, transcendentals=0),
    )


def shaped(*shape):
    return jax.ShapeDtypeStruct(shape, jnp.bfloat16)


def local(text, feats, count, proj, gain, q_weight, k_weight, v_weight):
    zh, zl, y = lax.axis_index("zh"), lax.axis_index("zl"), lax.axis_index("y")
    core, section = lax.axis_index("core"), lax.axis_index("section")

    turned = jnp.bitwise_xor(jnp.arange(CHIP_ROWS, dtype=jnp.int32), core * ROWS)
    position = ((zh * ZL + zl) * Y + y) * CHIP_ROWS + turned
    ladder = jnp.arange(HD // 2, dtype=jnp.float32) * 2.0 / HD
    angle = position.astype(jnp.float32)[:, None] * (ROPE_BASE ** (-ladder))[None, :]
    cosine = jnp.cos(angle)
    sine = jnp.sin(angle)
    cosine = jnp.concatenate([cosine, cosine], axis=-1)
    sine = jnp.concatenate([-sine, sine], axis=-1)
    gains = gain.astype(jnp.float32).reshape(SECTIONS, TP, 512)
    gains = jnp.where(section == 0, gains, gains[::-1]).reshape(8, 512)
    feats_b = swap(feats, "section")
    weight, spread = pl.pallas_call(
        join_kernel,
        out_shape=[shaped(64, 6 * HD), shaped(ZL * CORES, 64, 3 * HD)],
        in_specs=[pl.BlockSpec(memory_space=pl.ANY)] * 3,
        out_specs=[VMEM] * 2,
        scratch_shapes=[pltpu.SemaphoreType.DMA((3,))],
        cost_estimate=pl.CostEstimate(flops=0, bytes_accessed=800000, transcendentals=0),
    )(q_weight, k_weight, v_weight)
    weight_b = swap(weight, "zh")
    weight_a = lax.all_to_all(spread, ("zl", "core"), 0, 0, tiled=True)
    weight_a, weight_b, feats_b = lax.optimization_barrier((weight_a, weight_b, feats_b))
    (spread,) = call(spread_kernel, [shaped(ZL * CORES, 64, 3 * HD)], 0, 1, 1000, 1 << 20)(weight_b)
    weight_b = lax.all_to_all(spread, ("zl", "core"), 0, 0, tiled=True)

    feats = lax.all_gather(jnp.stack([feats, feats_b]), "tp", axis=0)
    weight_b, feats = lax.optimization_barrier((weight_b, feats))
    weight = lax.all_gather(jnp.stack([weight_a, weight_b]), "y", axis=0)
    (joined,) = call(join_frames_kernel, [shaped(ROWS, 512)], 1, 3, 2 * ROWS * 1024 * 512, 2 << 20)(
        jnp.stack([section, count[0]]), feats, proj.reshape(8, HD, 512), text
    )

    joined_b = swap(joined, "section")
    own_a = lax.all_gather(joined, "tp", axis=0)
    own_a, joined_b = lax.optimization_barrier((own_a, joined_b))
    other_a = swap(own_a, "core")
    own_b = lax.all_gather(joined_b, "tp", axis=0)
    other_b = swap(own_b, "core")
    queries, kv, lines = pl.pallas_call(
        project_kernel,
        out_shape=[
            shaped(CHIP_ROWS, HD),
            shaped(CHIP_ROWS, 2 * HD),
            shaped(ZL, CHIP_ROWS, 2 * HD),
        ],
        in_specs=[SMEM] + [VMEM] * 4 + [pl.BlockSpec(memory_space=pltpu.HBM)] + [VMEM] * 3,
        out_specs=[VMEM] * 3,
        scratch_shapes=[
            pltpu.VMEM((Y, ZH, ZL * CORES, 64, 3 * HD), jnp.bfloat16),
            pltpu.SemaphoreType.DMA((TP,)),
            pltpu.VMEM((SECTIONS * TP, CHIP_ROWS, 512), jnp.bfloat16),
        ],
        compiler_params=pltpu.CompilerParams(vmem_limit_bytes=LIMIT),
        cost_estimate=pl.CostEstimate(
            flops=2 * CHIP_ROWS * 4096 * 3 * HD, bytes_accessed=6 << 20, transcendentals=0
        ),
    )(
        jnp.bitwise_xor(zh, section).reshape(1),
        own_a,
        own_b,
        other_a,
        other_b,
        pltpu.with_memory_space_constraint(weight, pltpu.HBM),
        gains,
        cosine,
        sine,
    )

    kv_b = swap(kv, "zh")
    kv_a = lax.all_to_all(lines, "zl", 0, 0, tiled=True)
    queries = lax.all_gather(queries, "y", axis=0)
    kv_a, kv_b, queries = lax.optimization_barrier((kv_a, kv_b, queries))
    place = jnp.stack([zh, zl, y, core])
    scores = [pltpu.VMEM((Y, ZL, CHIP_ROWS, CHIP_ROWS), jnp.float32)]
    state = [jax.ShapeDtypeStruct((Y, CHIP_ROWS, HD), jnp.float32)] * 2
    flops = 4 * 1024 * 1024 * HD
    parts, levels = call(attend_own_kernel, state, 1, 2, flops, 2 << 20, scores)(
        place, queries, kv_a
    )
    kv_b = gather(kv_b, "zl", ZL)
    (parts,) = call(
        attend_rest_kernel, [shaped(Y * CORES, ROWS + 8, HD)], 1, 4, flops, 2 << 20, scores
    )(place, queries, kv_b, parts, levels)

    parts = lax.all_to_all(parts, ("y", "core"), 0, 0, tiled=True)
    (result,) = call(merge_kernel, [shaped(ROWS, 2 * HD)], 0, 1, 1 << 20, 1 << 20)(parts)
    return result


def solution(mesh):
    fine = Mesh(
        mesh.devices.reshape(ZH, ZL, Y, CORES, SECTIONS, TP),
        ("zh", "zl", "y", "core", "section", "tp"),
    )
    ctx = ("zh", "zl", "y", "core")
    in_specs = (P(ctx, F), P(ctx, F), P(ctx), P(None, F), P(), P(ctx, F), P(ctx, F), P(ctx, F))
    return jax.shard_map(
        local, mesh=fine, in_specs=in_specs, out_specs=P(ctx, F), check_vma=False
    )
```

```python
import math

import jax
import jax.numpy as jnp
from jax import lax
from jax.experimental import pallas as pl
from jax.experimental.pallas import tpu as pltpu
from jax.sharding import Mesh, PartitionSpec as P

HD = 128
ROPE_BASE = 1000000.0
NORM_EPS = 1e-05
MASKED = -1e30

ZH, ZL, Y, CORES, SECTIONS, TP = 2, 4, 4, 2, 2, 4
F = ("section", "tp")
ROWS = 128
CHIP_ROWS = 2 * ROWS
SWAP = [(0, 1), (1, 0)]
VMEM = pl.BlockSpec(memory_space=pltpu.VMEM)
SMEM = pl.BlockSpec(memory_space=pltpu.SMEM)
LIMIT = 40 << 20


def swap(v, axis):
    return lax.ppermute(v, axis, SWAP)


def gather(v, axis, n):
    return lax.all_to_all(jnp.broadcast_to(v[None], (n, *v.shape)), axis, 0, 0, tiled=True)


def join_frames_kernel(pick, feats, proj, text, out):
    vision = jnp.zeros((ROWS, 512), jnp.float32)
    for s in range(SECTIONS):
        first = jnp.bitwise_xor(pick[0], s) * TP
        for t in range(TP):
            vision = vision + jnp.dot(
                feats[t, s], proj[first + t], preferred_element_type=jnp.float32
            )
    row = lax.broadcasted_iota(jnp.int32, (ROWS, 512), 0)
    joined = jnp.where(row < pick[1], vision, text[...].astype(jnp.float32))
    out[...] = joined.astype(jnp.bfloat16)


def project_kernel(
    flip, own_a, own_b, other_a, other_b, stored, gain, cosine, sine, q_out, kv_out, lines_out, weight, sem, normed
):
    copies = [
        pltpu.make_async_copy(
            stored.at[:, :, t * CORES : (t + 1) * CORES],
            weight.at[:, :, t * CORES : (t + 1) * CORES],
            sem.at[t],
        )
        for t in range(TP)
    ]
    for copy in copies:
        copy.start()
    tiles = [(own, other, t) for own, other in ((own_a, other_a), (own_b, other_b)) for t in range(TP)]
    squares = jnp.zeros((CHIP_ROWS, 512), jnp.float32)
    for own, other, t in tiles:
        wide = jnp.concatenate([own[t], other[t]], axis=0).astype(jnp.float32)
        squares = squares + wide * wide
    mean_square = jnp.sum(squares, axis=-1, keepdims=True) * (1.0 / 4096)
    inverse = lax.rsqrt(mean_square + NORM_EPS)
    for i, (own, other, t) in enumerate(tiles):
        wide = jnp.concatenate([own[t], other[t]], axis=0).astype(jnp.float32)
        normed[i] = (wide * inverse * gain[i : i + 1, :]).astype(jnp.bfloat16)
    total = jnp.zeros((CHIP_ROWS, 3 * HD), jnp.float32)
    for i, (_, _, t) in enumerate(tiles):
        if i < TP:
            copies[i].wait()
        half = jnp.bitwise_xor(flip[0], i // TP)
        block = jnp.concatenate(
            [weight[y, half, t * CORES + c] for y in range(Y) for c in range(CORES)], axis=0
        )
        total = total + jnp.dot(normed[i], block, preferred_element_type=jnp.float32)
    q = total[:, :HD]
    k = total[:, HD : 2 * HD]
    cos, sin = cosine[...], sine[...]
    q_out[...] = (q * cos + pltpu.roll(q, HD // 2, 1) * sin).astype(jnp.bfloat16)
    k = (k * cos + pltpu.roll(k, HD // 2, 1) * sin).astype(jnp.bfloat16)
    v = total[:, 2 * HD :].astype(jnp.bfloat16)
    kv_out[:, :HD] = k
    kv_out[:, HD:] = v
    for i in range(ZL):
        lines_out[i, :, :HD] = k
        lines_out[i, :, HD:] = v


def encode(level):
    lane = lax.broadcasted_iota(jnp.int32, (CHIP_ROWS, HD), 1)
    high = level.astype(jnp.bfloat16).astype(jnp.float32)
    rest = level - high
    middle = rest.astype(jnp.bfloat16).astype(jnp.float32)
    low = rest - middle
    coded = jnp.where(
        lane == 0, high, jnp.where(lane == 1, middle, jnp.where(lane == 2, low, 0.0))
    ).astype(jnp.bfloat16)
    pick = lax.broadcasted_iota(jnp.int32, (8, HD), 0) == lax.broadcasted_iota(jnp.int32, (8, HD), 1)
    pick = pick.astype(jnp.float32).astype(jnp.bfloat16)
    coded = lax.dot_general(
        pick, coded, (((1,), (1,)), ((), ())), preferred_element_type=jnp.float32
    )
    return jnp.concatenate([coded[:, :ROWS], coded[:, ROWS:]], axis=0).astype(jnp.bfloat16)


def attend(q, kv, scores, mask):
    shape = (CHIP_ROWS, CHIP_ROWS)
    scale = 1.0 / math.sqrt(HD)
    peak = jnp.full(shape, MASKED, jnp.float32)
    for l in range(ZL):
        s = lax.dot_general(
            q, kv[l, :, :HD], (((1,), (1,)), ((), ())), preferred_element_type=jnp.float32
        )
        s = mask(l, s * scale)
        scores[l] = s
        peak = jnp.maximum(peak, s)
    best = jnp.max(peak, axis=-1, keepdims=True)
    mass = jnp.zeros(shape, jnp.float32)
    part = jnp.zeros((CHIP_ROWS, HD), jnp.float32)
    for l in range(ZL):
        w = jnp.exp(scores[l] - best)
        mass = mass + w
        part = part + jnp.dot(
            w.astype(jnp.bfloat16), kv[l, :, HD:], preferred_element_type=jnp.float32
        )
    total = jnp.sum(mass, axis=-1, keepdims=True)
    return part / total, jnp.where(best > 0.5 * MASKED, best + jnp.log(total), MASKED)


def attend_own_kernel(place, queries, kv, parts, levels, scores):
    zl, me, core = place[1], place[2], place[3]
    shape = (CHIP_ROWS, CHIP_ROWS)
    turn = core * ROWS
    row = jnp.bitwise_xor(lax.broadcasted_iota(jnp.int32, shape, 0), turn)
    col = jnp.bitwise_xor(lax.broadcasted_iota(jnp.int32, shape, 1), turn)
    ahead = col - row

    def one(pair, carry):
        for i in range(2):
            y = pair * 2 + i

            def mask(l, s):
                return jnp.where(ahead <= ((zl - l) * Y + y - me) * CHIP_ROWS, s, MASKED)

            part, level = attend(queries[y], kv, scores.at[i], mask)
            parts[y] = part
            levels[y] = jnp.broadcast_to(level, (CHIP_ROWS, HD))
        return carry

    lax.fori_loop(0, Y // 2, one, 0)


def attend_rest_kernel(place, queries, kv, parts, levels, out, scores):
    def put(y, part, level):
        coded = encode(level)
        part = part.astype(jnp.bfloat16)
        for i in range(CORES):
            owner = y * CORES + jnp.bitwise_xor(place[3], i)
            out[owner, :ROWS, :] = part[i * ROWS : (i + 1) * ROWS]
            out[owner, ROWS:, :] = coded[i * 8 : (i + 1) * 8]

    @pl.when(place[0] == 0)
    def _():
        for y in range(Y):
            put(y, parts[y], levels[y, :, 0:1])

    @pl.when(place[0] != 0)
    def _():
        for y in range(Y):
            part, level = attend(queries[y], kv, scores.at[y], lambda l, s: s)
            before = levels[y, :, 0:1]
            top = jnp.maximum(level, before)
            new, old = jnp.exp(level - top), jnp.exp(before - top)
            total = new + old
            put(y, (part * new + parts[y] * old) / total, top + jnp.log(total))


def merge_kernel(parts, out):
    shares = []
    for h in range(CORES):
        levels = []
        for y in range(Y):
            coded = parts[y * CORES + h, ROWS:, :].astype(jnp.float32)
            levels.append(coded[0:1] + coded[1:2] + coded[2:3])
        levels = jnp.concatenate(levels, axis=0)
        share = jnp.exp(levels - jnp.max(levels, axis=0, keepdims=True))
        shares.append(share / jnp.sum(share, axis=0, keepdims=True))
    shares = jnp.transpose(jnp.concatenate(shares * (ROWS // (CORES * Y)), axis=0))
    for h in range(CORES):
        result = jnp.zeros((ROWS, HD), jnp.float32)
        for y in range(Y):
            lane = h * Y + y
            block = parts[y * CORES + h, :ROWS, :].astype(jnp.float32)
            result = result + shares[:, lane : lane + 1] * block
        out[:, h * HD : (h + 1) * HD] = result.astype(jnp.bfloat16)


def spread_kernel(w, out):
    for h in range(CORES):
        for i in range(3):
            block = w[:, (2 * i + h) * HD : (2 * i + h + 1) * HD]
            for l in range(ZL):
                out[l * CORES + h, :, i * HD : (i + 1) * HD] = block


def join_kernel(q, k, v, joined, out, sems):
    copies = [
        pltpu.make_async_copy(w, joined.at[:, i * 2 * HD : (i + 1) * 2 * HD], sems.at[i])
        for i, w in enumerate((q, k, v))
    ]
    for copy in copies:
        copy.start()
    for copy in copies:
        copy.wait()
    spread_kernel(joined, out)


def call(kernel, outs, n_scalars, n_arrays, flops, size, scratch=()):
    return pl.pallas_call(
        kernel,
        out_shape=outs,
        in_specs=[SMEM] * n_scalars + [VMEM] * n_arrays,
        out_specs=[VMEM] * len(outs),
        scratch_shapes=list(scratch),
        compiler_params=pltpu.CompilerParams(vmem_limit_bytes=LIMIT),
        cost_estimate=pl.CostEstimate(flops=flops, bytes_accessed=size, transcendentals=0),
    )


def shaped(*shape):
    return jax.ShapeDtypeStruct(shape, jnp.bfloat16)


def local(text, feats, count, proj, gain, q_weight, k_weight, v_weight):
    zh, zl, y = lax.axis_index("zh"), lax.axis_index("zl"), lax.axis_index("y")
    core, section = lax.axis_index("core"), lax.axis_index("section")

    turned = jnp.bitwise_xor(jnp.arange(CHIP_ROWS, dtype=jnp.int32), core * ROWS)
    position = ((zh * ZL + zl) * Y + y) * CHIP_ROWS + turned
    ladder = jnp.arange(HD // 2, dtype=jnp.float32) * 2.0 / HD
    angle = position.astype(jnp.float32)[:, None] * (ROPE_BASE ** (-ladder))[None, :]
    cosine = jnp.cos(angle)
    sine = jnp.sin(angle)
    cosine = jnp.concatenate([cosine, cosine], axis=-1)
    sine = jnp.concatenate([-sine, sine], axis=-1)
    gains = gain.astype(jnp.float32).reshape(SECTIONS, TP, 512)
    gains = jnp.where(section == 0, gains, gains[::-1]).reshape(8, 512)
    feats_b = swap(feats, "section")
    weight, spread = pl.pallas_call(
        join_kernel,
        out_shape=[shaped(64, 6 * HD), shaped(ZL * CORES, 64, 3 * HD)],
        in_specs=[pl.BlockSpec(memory_space=pl.ANY)] * 3,
        out_specs=[VMEM] * 2,
        scratch_shapes=[pltpu.SemaphoreType.DMA((3,))],
        cost_estimate=pl.CostEstimate(flops=0, bytes_accessed=800000, transcendentals=0),
    )(q_weight, k_weight, v_weight)
    weight_b = swap(weight, "zh")
    weight_a = lax.all_to_all(spread, ("zl", "core"), 0, 0, tiled=True)
    weight_a, weight_b, feats_b = lax.optimization_barrier((weight_a, weight_b, feats_b))
    (spread,) = call(spread_kernel, [shaped(ZL * CORES, 64, 3 * HD)], 0, 1, 1000, 1 << 20)(weight_b)
    weight_b = lax.all_to_all(spread, ("zl", "core"), 0, 0, tiled=True)

    feats = lax.all_gather(jnp.stack([feats, feats_b]), "tp", axis=0)
    weight_b, feats = lax.optimization_barrier((weight_b, feats))
    weight = lax.all_gather(jnp.stack([weight_a, weight_b]), "y", axis=0)
    (joined,) = call(join_frames_kernel, [shaped(ROWS, 512)], 1, 3, 2 * ROWS * 1024 * 512, 2 << 20)(
        jnp.stack([section, count[0]]), feats, proj.reshape(8, HD, 512), text
    )

    joined_b = swap(joined, "section")
    own_a = lax.all_gather(joined, "tp", axis=0)
    own_a, joined_b = lax.optimization_barrier((own_a, joined_b))
    other_a = swap(own_a, "core")
    own_b = lax.all_gather(joined_b, "tp", axis=0)
    other_b = swap(own_b, "core")
    queries, kv, lines = pl.pallas_call(
        project_kernel,
        out_shape=[
            shaped(CHIP_ROWS, HD),
            shaped(CHIP_ROWS, 2 * HD),
            shaped(ZL, CHIP_ROWS, 2 * HD),
        ],
        in_specs=[SMEM] + [VMEM] * 4 + [pl.BlockSpec(memory_space=pltpu.HBM)] + [VMEM] * 3,
        out_specs=[VMEM] * 3,
        scratch_shapes=[
            pltpu.VMEM((Y, ZH, ZL * CORES, 64, 3 * HD), jnp.bfloat16),
            pltpu.SemaphoreType.DMA((TP,)),
            pltpu.VMEM((SECTIONS * TP, CHIP_ROWS, 512), jnp.bfloat16),
        ],
        compiler_params=pltpu.CompilerParams(vmem_limit_bytes=LIMIT),
        cost_estimate=pl.CostEstimate(
            flops=2 * CHIP_ROWS * 4096 * 3 * HD, bytes_accessed=6 << 20, transcendentals=0
        ),
    )(
        jnp.bitwise_xor(zh, section).reshape(1),
        own_a,
        own_b,
        other_a,
        other_b,
        pltpu.with_memory_space_constraint(weight, pltpu.HBM),
        gains,
        cosine,
        sine,
    )

    kv_b = swap(kv, "zh")
    kv_a = lax.all_to_all(lines, "zl", 0, 0, tiled=True)
    queries = lax.all_gather(queries, "y", axis=0)
    kv_a, kv_b, queries = lax.optimization_barrier((kv_a, kv_b, queries))
    place = jnp.stack([zh, zl, y, core])
    scores = [pltpu.VMEM((Y, ZL, CHIP_ROWS, CHIP_ROWS), jnp.float32)]
    state = [jax.ShapeDtypeStruct((Y, CHIP_ROWS, HD), jnp.float32)] * 2
    flops = 4 * 1024 * 1024 * HD
    parts, levels = call(attend_own_kernel, state, 1, 2, flops, 2 << 20, scores)(
        place, queries, kv_a
    )
    kv_b = gather(kv_b, "zl", ZL)
    (parts,) = call(
        attend_rest_kernel, [shaped(Y * CORES, ROWS + 8, HD)], 1, 4, flops, 2 << 20, scores
    )(place, queries, kv_b, parts, levels)

    parts = lax.all_to_all(parts, ("y", "core"), 0, 0, tiled=True)
    (result,) = call(merge_kernel, [shaped(ROWS, 2 * HD)], 0, 1, 1 << 20, 1 << 20)(parts)
    return result


def solution(mesh):
    fine = Mesh(
        mesh.devices.reshape(ZH, ZL, Y, CORES, SECTIONS, TP),
        ("zh", "zl", "y", "core", "section", "tp"),
    )
    ctx = ("zh", "zl", "y", "core")
    in_specs = (P(ctx, F), P(ctx, F), P(ctx), P(None, F), P(), P(ctx, F), P(ctx, F), P(ctx, F))
    return jax.shard_map(
        local, mesh=fine, in_specs=in_specs, out_specs=P(ctx, F), check_vma=False
    )
```

```python
import math

import jax
import jax.numpy as jnp
from jax import lax
from jax.experimental import pallas as pl
from jax.experimental.pallas import tpu as pltpu
from jax.sharding import Mesh, PartitionSpec as P

HD = 128
ROPE_BASE = 1000000.0
NORM_EPS = 1e-05
MASKED = -1e30

ZH, ZL, Y, CORES, SECTIONS, TP = 2, 4, 4, 2, 2, 4
F = ("section", "tp")
ROWS = 128
CHIP_ROWS = 2 * ROWS
SWAP = [(0, 1), (1, 0)]
VMEM = pl.BlockSpec(memory_space=pltpu.VMEM)
SMEM = pl.BlockSpec(memory_space=pltpu.SMEM)
LIMIT = 40 << 20


def swap(v, axis):
    return lax.ppermute(v, axis, SWAP)


def gather(v, axis, n):
    return lax.all_to_all(jnp.broadcast_to(v[None], (n, *v.shape)), axis, 0, 0, tiled=True)


def join_frames_kernel(pick, feats, proj, text, out):
    vision = jnp.zeros((ROWS, 512), jnp.float32)
    for s in range(SECTIONS):
        first = jnp.bitwise_xor(pick[0], s) * TP
        for t in range(TP):
            vision = vision + jnp.dot(
                feats[t, s], proj[first + t], preferred_element_type=jnp.float32
            )
    row = lax.broadcasted_iota(jnp.int32, (ROWS, 512), 0)
    joined = jnp.where(row < pick[1], vision, text[...].astype(jnp.float32))
    out[...] = joined.astype(jnp.bfloat16)


def project_kernel(
    flip, own_a, own_b, other_a, other_b, stored, gain, cosine, sine, q_out, kv_out, weight, sem, normed
):
    copies = [
        pltpu.make_async_copy(
            stored.at[:, :, t * CORES : (t + 1) * CORES],
            weight.at[:, :, t * CORES : (t + 1) * CORES],
            sem.at[t],
        )
        for t in range(TP)
    ]
    for copy in copies:
        copy.start()
    tiles = [(own, other, t) for own, other in ((own_a, other_a), (own_b, other_b)) for t in range(TP)]
    squares = jnp.zeros((CHIP_ROWS, 512), jnp.float32)
    for own, other, t in tiles:
        wide = jnp.concatenate([own[t], other[t]], axis=0).astype(jnp.float32)
        squares = squares + wide * wide
    mean_square = jnp.sum(squares, axis=-1, keepdims=True) * (1.0 / 4096)
    inverse = lax.rsqrt(mean_square + NORM_EPS)
    for i, (own, other, t) in enumerate(tiles):
        wide = jnp.concatenate([own[t], other[t]], axis=0).astype(jnp.float32)
        normed[i] = (wide * inverse * gain[i : i + 1, :]).astype(jnp.bfloat16)
    for copy in copies:
        copy.wait()
    total = jnp.zeros((CHIP_ROWS, 3 * HD), jnp.float32)
    for i, (_, _, t) in enumerate(tiles):
        half = jnp.bitwise_xor(flip[0], i // TP)
        block = jnp.concatenate(
            [weight[y, half, t * CORES + c] for y in range(Y) for c in range(CORES)], axis=0
        )
        total = total + jnp.dot(normed[i], block, preferred_element_type=jnp.float32)
    q = total[:, :HD]
    k = total[:, HD : 2 * HD]
    cos, sin = cosine[...], sine[...]
    q_out[...] = (q * cos + pltpu.roll(q, HD // 2, 1) * sin).astype(jnp.bfloat16)
    k = (k * cos + pltpu.roll(k, HD // 2, 1) * sin).astype(jnp.bfloat16)
    v = total[:, 2 * HD :].astype(jnp.bfloat16)
    kv_out[:, :HD] = k
    kv_out[:, HD:] = v


def encode(level):
    lane = lax.broadcasted_iota(jnp.int32, (CHIP_ROWS, HD), 1)
    high = level.astype(jnp.bfloat16).astype(jnp.float32)
    rest = level - high
    middle = rest.astype(jnp.bfloat16).astype(jnp.float32)
    low = rest - middle
    coded = jnp.where(
        lane == 0, high, jnp.where(lane == 1, middle, jnp.where(lane == 2, low, 0.0))
    ).astype(jnp.bfloat16)
    pick = lax.broadcasted_iota(jnp.int32, (8, HD), 0) == lax.broadcasted_iota(jnp.int32, (8, HD), 1)
    pick = pick.astype(jnp.float32).astype(jnp.bfloat16)
    coded = lax.dot_general(
        pick, coded, (((1,), (1,)), ((), ())), preferred_element_type=jnp.float32
    )
    return jnp.concatenate([coded[:, :ROWS], coded[:, ROWS:]], axis=0).astype(jnp.bfloat16)


def attend(q, kv, scores, mask):
    shape = (CHIP_ROWS, CHIP_ROWS)
    scale = 1.0 / math.sqrt(HD)
    peak = jnp.full(shape, MASKED, jnp.float32)
    for l in range(ZL):
        s = lax.dot_general(
            q, kv[l, :, :HD], (((1,), (1,)), ((), ())), preferred_element_type=jnp.float32
        )
        s = mask(l, s * scale)
        scores[l] = s
        peak = jnp.maximum(peak, s)
    best = jnp.max(peak, axis=-1, keepdims=True)
    mass = jnp.zeros(shape, jnp.float32)
    part = jnp.zeros((CHIP_ROWS, HD), jnp.float32)
    for l in range(ZL):
        w = jnp.exp(scores[l] - best)
        mass = mass + w
        part = part + jnp.dot(
            w.astype(jnp.bfloat16), kv[l, :, HD:], preferred_element_type=jnp.float32
        )
    total = jnp.sum(mass, axis=-1, keepdims=True)
    return part / total, jnp.where(best > 0.5 * MASKED, best + jnp.log(total), MASKED)


def attend_own_kernel(place, queries, kv, parts, levels, scores):
    zl, me, core = place[1], place[2], place[3]
    shape = (CHIP_ROWS, CHIP_ROWS)
    turn = core * ROWS
    row = jnp.bitwise_xor(lax.broadcasted_iota(jnp.int32, shape, 0), turn)
    col = jnp.bitwise_xor(lax.broadcasted_iota(jnp.int32, shape, 1), turn)
    ahead = col - row

    def one(pair, carry):
        for i in range(2):
            y = pair * 2 + i

            def mask(l, s):
                return jnp.where(ahead <= ((zl - l) * Y + y - me) * CHIP_ROWS, s, MASKED)

            part, level = attend(queries[y], kv, scores.at[i], mask)
            parts[y] = part
            levels[y] = jnp.broadcast_to(level, (CHIP_ROWS, HD))
        return carry

    lax.fori_loop(0, Y // 2, one, 0)


def attend_rest_kernel(place, queries, kv, parts, levels, out, scores):
    def put(y, part, level):
        coded = encode(level)
        part = part.astype(jnp.bfloat16)
        for i in range(CORES):
            owner = y * CORES + jnp.bitwise_xor(place[3], i)
            out[owner, :ROWS, :] = part[i * ROWS : (i + 1) * ROWS]
            out[owner, ROWS:, :] = coded[i * 8 : (i + 1) * 8]

    @pl.when(place[0] == 0)
    def _():
        for y in range(Y):
            put(y, parts[y], levels[y, :, 0:1])

    @pl.when(place[0] != 0)
    def _():
        for y in range(Y):
            part, level = attend(queries[y], kv, scores.at[y], lambda l, s: s)
            before = levels[y, :, 0:1]
            top = jnp.maximum(level, before)
            new, old = jnp.exp(level - top), jnp.exp(before - top)
            total = new + old
            put(y, (part * new + parts[y] * old) / total, top + jnp.log(total))


def merge_kernel(parts, out):
    shares = []
    for h in range(CORES):
        levels = []
        for y in range(Y):
            coded = parts[y * CORES + h, ROWS:, :].astype(jnp.float32)
            levels.append(coded[0:1] + coded[1:2] + coded[2:3])
        levels = jnp.concatenate(levels, axis=0)
        share = jnp.exp(levels - jnp.max(levels, axis=0, keepdims=True))
        shares.append(share / jnp.sum(share, axis=0, keepdims=True))
    shares = jnp.transpose(jnp.concatenate(shares * (ROWS // (CORES * Y)), axis=0))
    for h in range(CORES):
        result = jnp.zeros((ROWS, HD), jnp.float32)
        for y in range(Y):
            lane = h * Y + y
            block = parts[y * CORES + h, :ROWS, :].astype(jnp.float32)
            result = result + shares[:, lane : lane + 1] * block
        out[:, h * HD : (h + 1) * HD] = result.astype(jnp.bfloat16)


def spread_kernel(w, out):
    for h in range(CORES):
        for i in range(3):
            block = w[:, (2 * i + h) * HD : (2 * i + h + 1) * HD]
            for l in range(ZL):
                out[l * CORES + h, :, i * HD : (i + 1) * HD] = block


def join_kernel(q, k, v, joined, out, sems):
    copies = [
        pltpu.make_async_copy(w, joined.at[:, i * 2 * HD : (i + 1) * 2 * HD], sems.at[i])
        for i, w in enumerate((q, k, v))
    ]
    for copy in copies:
        copy.start()
    for copy in copies:
        copy.wait()
    spread_kernel(joined, out)


def call(kernel, outs, n_scalars, n_arrays, flops, size, scratch=()):
    return pl.pallas_call(
        kernel,
        out_shape=outs,
        in_specs=[SMEM] * n_scalars + [VMEM] * n_arrays,
        out_specs=[VMEM] * len(outs),
        scratch_shapes=list(scratch),
        compiler_params=pltpu.CompilerParams(vmem_limit_bytes=LIMIT),
        cost_estimate=pl.CostEstimate(flops=flops, bytes_accessed=size, transcendentals=0),
    )


def shaped(*shape):
    return jax.ShapeDtypeStruct(shape, jnp.bfloat16)


def local(text, feats, count, proj, gain, q_weight, k_weight, v_weight):
    zh, zl, y = lax.axis_index("zh"), lax.axis_index("zl"), lax.axis_index("y")
    core, section = lax.axis_index("core"), lax.axis_index("section")

    turned = jnp.bitwise_xor(jnp.arange(CHIP_ROWS, dtype=jnp.int32), core * ROWS)
    position = ((zh * ZL + zl) * Y + y) * CHIP_ROWS + turned
    ladder = jnp.arange(HD // 2, dtype=jnp.float32) * 2.0 / HD
    angle = position.astype(jnp.float32)[:, None] * (ROPE_BASE ** (-ladder))[None, :]
    cosine = jnp.cos(angle)
    sine = jnp.sin(angle)
    cosine = jnp.concatenate([cosine, cosine], axis=-1)
    sine = jnp.concatenate([-sine, sine], axis=-1)
    gains = gain.astype(jnp.float32).reshape(SECTIONS, TP, 512)
    gains = jnp.where(section == 0, gains, gains[::-1]).reshape(8, 512)
    feats_b = swap(feats, "section")
    weight, spread = pl.pallas_call(
        join_kernel,
        out_shape=[shaped(64, 6 * HD), shaped(ZL * CORES, 64, 3 * HD)],
        in_specs=[pl.BlockSpec(memory_space=pl.ANY)] * 3,
        out_specs=[VMEM] * 2,
        scratch_shapes=[pltpu.SemaphoreType.DMA((3,))],
        cost_estimate=pl.CostEstimate(flops=0, bytes_accessed=800000, transcendentals=0),
    )(q_weight, k_weight, v_weight)
    weight_b = swap(weight, "zh")
    weight_a = lax.all_to_all(spread, ("zl", "core"), 0, 0, tiled=True)
    weight_a, weight_b, feats_b = lax.optimization_barrier((weight_a, weight_b, feats_b))
    (spread,) = call(spread_kernel, [shaped(ZL * CORES, 64, 3 * HD)], 0, 1, 1000, 1 << 20)(weight_b)
    weight_b = lax.all_to_all(spread, ("zl", "core"), 0, 0, tiled=True)

    feats = lax.all_gather(jnp.stack([feats, feats_b]), "tp", axis=0)
    weight_b, feats = lax.optimization_barrier((weight_b, feats))
    weight = lax.all_gather(jnp.stack([weight_a, weight_b]), "y", axis=0)
    (joined,) = call(join_frames_kernel, [shaped(ROWS, 512)], 1, 3, 2 * ROWS * 1024 * 512, 2 << 20)(
        jnp.stack([section, count[0]]), feats, proj.reshape(8, HD, 512), text
    )

    joined_b = swap(joined, "section")
    own_a = lax.all_gather(joined, "tp", axis=0)
    own_a, joined_b = lax.optimization_barrier((own_a, joined_b))
    other_a = swap(own_a, "core")
    own_b = lax.all_gather(joined_b, "tp", axis=0)
    other_b = swap(own_b, "core")
    queries, kv = pl.pallas_call(
        project_kernel,
        out_shape=[
            shaped(CHIP_ROWS, HD),
            shaped(CHIP_ROWS, 2 * HD),
        ],
        in_specs=[SMEM] + [VMEM] * 4 + [pl.BlockSpec(memory_space=pltpu.HBM)] + [VMEM] * 3,
        out_specs=[VMEM] * 2,
        scratch_shapes=[
            pltpu.VMEM((Y, ZH, ZL * CORES, 64, 3 * HD), jnp.bfloat16),
            pltpu.SemaphoreType.DMA((TP,)),
            pltpu.VMEM((SECTIONS * TP, CHIP_ROWS, 512), jnp.bfloat16),
        ],
        compiler_params=pltpu.CompilerParams(vmem_limit_bytes=LIMIT),
        cost_estimate=pl.CostEstimate(
            flops=2 * CHIP_ROWS * 4096 * 3 * HD, bytes_accessed=6 << 20, transcendentals=0
        ),
    )(
        jnp.bitwise_xor(zh, section).reshape(1),
        own_a,
        own_b,
        other_a,
        other_b,
        pltpu.with_memory_space_constraint(weight, pltpu.HBM),
        gains,
        cosine,
        sine,
    )

    kv_b = swap(kv, "zh")
    kv_a = gather(kv, "zl", ZL)
    queries = lax.all_gather(queries, "y", axis=0)
    kv_a, kv_b, queries = lax.optimization_barrier((kv_a, kv_b, queries))
    place = jnp.stack([zh, zl, y, core])
    scores = [pltpu.VMEM((Y, ZL, CHIP_ROWS, CHIP_ROWS), jnp.float32)]
    state = [jax.ShapeDtypeStruct((Y, CHIP_ROWS, HD), jnp.float32)] * 2
    flops = 4 * 1024 * 1024 * HD
    parts, levels = call(attend_own_kernel, state, 1, 2, flops, 2 << 20, scores)(
        place, queries, kv_a
    )
    kv_b = gather(kv_b, "zl", ZL)
    (parts,) = call(
        attend_rest_kernel, [shaped(Y * CORES, ROWS + 8, HD)], 1, 4, flops, 2 << 20, scores
    )(place, queries, kv_b, parts, levels)

    parts = lax.all_to_all(parts, ("y", "core"), 0, 0, tiled=True)
    (result,) = call(merge_kernel, [shaped(ROWS, 2 * HD)], 0, 1, 1 << 20, 1 << 20)(parts)
    return result


def solution(mesh):
    fine = Mesh(
        mesh.devices.reshape(ZH, ZL, Y, CORES, SECTIONS, TP),
        ("zh", "zl", "y", "core", "section", "tp"),
    )
    ctx = ("zh", "zl", "y", "core")
    in_specs = (P(ctx, F), P(ctx, F), P(ctx), P(None, F), P(), P(ctx, F), P(ctx, F), P(ctx, F))
    return jax.shard_map(
        local, mesh=fine, in_specs=in_specs, out_specs=P(ctx, F), check_vma=False
    )
```
